32 devices in a mesh: dp: 8 (over y, x, core), tp: 4 (over z).
Axes of the slice: x: 2, y: 2, z: 4, core: 2. Of those that a mesh axis runs over, the one named last changes fastest.
Arguments:
- tokens: bfloat16 [16384, 2048], P('dp'), may hold values from -6 to 6
- doc_ids: int32 [16, 1024], P('dp'), may hold values from 0 to 3, never falling along the last dimension, each value on 1 to 512 neighbouring positions
- norm1_gain: bfloat16 [2048], replicated, may hold values from 0.5 to 1.5
- norm1_bias: bfloat16 [2048], replicated, may hold values from -4 to 4
- query_weight: bfloat16 [2048, 2048], P(None, 'tp'), may hold values from -0.125 to 0.125
- query_bias: bfloat16 [2048], P('tp'), may hold values from -6 to 6
- keyval_weight: bfloat16 [2048, 256], replicated, may hold values from -0.125 to 0.125
- value_bias: bfloat16 [128], replicated, may hold values from -3 to 3
- out_weight: bfloat16 [2048, 2048], P('tp'), may hold values from -0.5 to 0.5
- out_bias: bfloat16 [2048], replicated, may hold values from -6 to 6
- norm2_gain: bfloat16 [2048], replicated, may hold values from 0.5 to 1.5
- norm2_bias: bfloat16 [2048], replicated, may hold values from -4 to 4
- up_weight: bfloat16 [2048, 8192], P(None, 'tp'), may hold values from -0.125 to 0.125
- up_bias: bfloat16 [8192], P('tp'), may hold values from -6 to 6
- down_weight: bfloat16 [8192, 2048], P('tp'), may hold values from -0.0625 to 0.0625
- down_bias: bfloat16 [2048], replicated, may hold values from -6 to 6
- grad_out: bfloat16 [16384, 2048], P('dp'), may hold values from -6 to 6
Outputs:
- output: bfloat16 [16384, 2048], P('dp')
- grad_tokens: bfloat16 [16384, 2048], P('dp')
- grad_norm1_gain: float32 [2048], P('dp')
- grad_norm1_bias: float32 [2048], P('dp')
- grad_query_weight: float32 [2048, 2048], P('dp', 'tp')
- grad_query_bias: float32 [2048], P(('tp', 'dp'))
- grad_keyval_weight: float32 [2048, 256], P(('dp', 'tp'))
- grad_value_bias: float32 [128], P(('dp', 'tp'))
- grad_out_weight: float32 [2048, 2048], P('tp', 'dp')
- grad_out_bias: float32 [2048], P('dp')
- grad_norm2_gain: float32 [2048], P('dp')
- grad_norm2_bias: float32 [2048], P('dp')
- grad_up_weight: float32 [2048, 8192], P('dp', 'tp')
- grad_up_bias: float32 [8192], P(('tp', 'dp'))
- grad_down_weight: float32 [8192, 2048], P('tp', 'dp')
- grad_down_bias: float32 [2048], P('dp')
The draws below stay inside these ranges and needn't reach their ends.
Inputs may be any that keep to these rules, and one draw needn't show every extreme that they name: `doc_ids`: document numbers never fall along a row of a window; a document spans 1 to half of 1024 tokens.
All inputs are finite; a program needn't handle non-finite values.
Results may differ from the reference program's by a relative error of at most 0.02.
Values may be sent and summed in bfloat16 or wider, within the bound.
A program may use at most 384 MiB of HBM per device.

```python
import math
import jax
import jax.numpy as jnp
import numpy as np
from jax import lax

D = 2048
NQ = 16
HD = 128
FF = 8192
SEQ = 1024
DOCS = 4
SEQUENCES = 16
TOKENS = 16384
N_TP = 4


def spiked(drawn, stream_key, source, target, shards_of, factor):
    def block_of(dim):
        return (jnp.arange(drawn.shape[dim]) // (drawn.shape[dim] // shards_of)).reshape((-1,) + (1,) * (drawn.ndim - 1 - dim))

    near = jax.random.permutation(stream_key, shards_of)[block_of(target)]
    other_side = (block_of(target) + shards_of // 2) % shards_of
    return jnp.where((block_of(source) == near) | (block_of(source) == other_side), factor * drawn, drawn)


def block_scale(own_key, dims, pieces, smallest, high):
    factor_of = 1.0
    for axis_at, shards_of in pieces:
        steps = jax.random.uniform(jax.random.fold_in(jax.random.fold_in(own_key, 6), axis_at), (shards_of,), jnp.float32, smallest / len(pieces), high / len(pieces))
        factor_of = factor_of * jnp.repeat(jnp.exp(steps), dims[axis_at] // shards_of).reshape((-1,) + (1,) * (len(dims) - 1 - axis_at))
    return factor_of


def split_up(number_of, total, most, slope):
    portions = [(1 << 20) // math.isqrt(standing ** slope) + 1 for standing in range(2, number_of + 1)]
    rest, counts = total - most - (number_of - 1), [1] * (number_of - 1)
    while rest > 0:
        free = [i for i in range(number_of - 1) if counts[i] < most]
        pool, budget = sum([portions[i] for i in free]), rest
        for i in free:
            addition = min(most - counts[i], max(1, budget * portions[i] // pool), rest)
            counts[i] = counts[i] + addition
            rest = rest - addition
    return np.array([most] + counts)


def uneven(key, amount, total, reach, slope):
    if amount == 2:
        one = jax.random.randint(key, (), max(1, total - reach), min(reach, total - 1) + 1)
        return jnp.stack([one, total - one])
    lengths = jnp.asarray(split_up(amount, total, reach, slope), jnp.int32)
    pairs = (amount - 1) // 2
    donor, receiver = lengths[1:1 + 2 * pairs:2], lengths[2:2 + 2 * pairs:2]
    room = jnp.minimum(donor - 1, reach - receiver)
    shifted = jax.random.randint(jax.random.fold_in(key, 1), (pairs,), 0, 1 << 20) % (room + 1)
    lengths = lengths.at[1:1 + 2 * pairs:2].set(donor - shifted).at[2:2 + 2 * pairs:2].set(receiver + shifted)
    return lengths[jax.random.permutation(jax.random.fold_in(key, 2), amount)]


def noise(stream_key, extent, scale, limit, pieces=(), dtype=jnp.bfloat16):
    drawn = scale * jax.random.normal(stream_key, extent, jnp.float32)
    if pieces:
        drawn = drawn * block_scale(stream_key, extent, pieces, -0.22, 0.18)
    return jnp.clip(drawn, -limit, limit).astype(dtype)


def heavy_noise(stream_key, extent, width, limit, cuts, heavy, kind=jnp.bfloat16):
    drawn = width * jax.random.normal(stream_key, extent, jnp.float32)
    if cuts:
        drawn = drawn * block_scale(stream_key, extent, cuts, -0.22, 0.18)
    return jnp.clip(spiked(drawn, jax.random.fold_in(stream_key, 3), *heavy), -limit, limit).astype(kind)


def setup_inputs(seed: int = 0) -> dict:
    splits = jax.random.split(jax.random.key(seed), 18)
    return {
        "tokens": noise(splits[0], (TOKENS, D), 1.0, 6.0, ((0, 8),)),
        "doc_ids": jax.vmap(lambda own: jnp.searchsorted(jnp.cumsum(uneven(own, DOCS, SEQ, SEQ // 2, 1)), jnp.arange(SEQ), side="right"))(jax.random.split(splits[1], SEQUENCES)).reshape((SEQUENCES, SEQ)).astype(jnp.int32),
        "norm1_gain": jnp.clip(1.0 + 0.1 * jax.random.normal(splits[2], (D,), jnp.float32), 0.5, 1.5).astype(jnp.bfloat16),
        "norm1_bias": noise(splits[3], (D,), 0.3, 4.0),
        "query_weight": noise(splits[4], (D, NQ * HD), D ** -0.5, 0.125, ((1, 4),)),
        "query_bias": noise(splits[5], (NQ * HD,), 0.5, 6.0, ((0, 4),)),
        "keyval_weight": noise(splits[6], (D, 2 * HD), D ** -0.5, 0.125),
        "value_bias": noise(splits[7], (HD,), 0.2, 3.0),
        "out_weight": noise(splits[8], (NQ * HD, D), (NQ * HD // 16) ** -0.5, 0.5, ((0, 4),)),
        "out_bias": noise(splits[9], (D,), 0.5, 6.0),
        "norm2_gain": jnp.clip(1.0 + 0.1 * jax.random.normal(splits[10], (D,), jnp.float32), 0.5, 1.5).astype(jnp.bfloat16),
        "norm2_bias": noise(splits[11], (D,), 0.3, 4.0),
        "up_weight": noise(splits[12], (D, FF), D ** -0.5, 0.125, ((1, 4),)),
        "up_bias": noise(splits[13], (FF,), 0.5, 6.0, ((0, 4),)),
        "down_weight": noise(splits[14], (FF, D), FF ** -0.5, 0.0625, ((0, 4),)),
        "down_bias": noise(splits[15], (D,), 0.5, 6.0),
        "grad_out": heavy_noise(splits[16], (TOKENS, D), 1.0, 6.0, ((0, 8),), (0, 1, 8, 2.0)),
    }


@jax.custom_vjp
def low(v):
    return lax.optimization_barrier(v.astype(jnp.bfloat16)).astype(jnp.float32)

@jax.custom_vjp
def low_back(v):
    return v

def low_keep(v):
    return (low(v), None)

def low_pass(kept, grad):
    return (grad,)

def back_keep(v):
    return (v, None)

def back_low(kept, grad):
    return (low(grad),)
low.defvjp(low_keep, low_pass)
low_back.defvjp(back_keep, back_low)

def both_round(values):
    return low_back(low(values))

def product(form, operand_a, operand_b):
    return jnp.einsum(form, operand_a, operand_b, precision=lax.Precision.HIGHEST)

def layer_norm(values, gain_vec, shift_vec):
    center = values - lax.optimization_barrier(jnp.mean(values, axis=-1, keepdims=True))
    spread = lax.optimization_barrier(jnp.mean(center * center, axis=-1, keepdims=True))
    return center * lax.rsqrt(spread + 1e-05) * gain_vec + shift_vec

def block_forward(params, seq_rows, doc_row):
    norm1_gain, norm1_bias, query_weight, query_bias, keyval_weight, value_bias, out_weight, out_bias, norm2_gain, norm2_bias, up_weight, up_bias, down_weight, down_bias = params
    local_heads = NQ // N_TP
    local_units = FF // N_TP
    normed1 = low(layer_norm(seq_rows, norm1_gain, norm1_bias))
    copies1 = low_back(jnp.broadcast_to(normed1, (N_TP, SEQ, D)))
    query_groups = query_weight.reshape(D, N_TP, local_heads * HD).transpose(1, 0, 2)
    queries = both_round(product('gsd,gde->gse', copies1, query_groups) + query_bias.reshape(N_TP, 1, local_heads * HD))
    keyval = product('gsd,de->gse', copies1, keyval_weight)
    keys_low = both_round(keyval[:, :, :HD])
    values_low = both_round(keyval[:, :, HD:] + value_bias)
    heads_q = queries.reshape(N_TP, SEQ, local_heads, HD)
    scores = low_back(product('gshd,gtd->ghst', heads_q, keys_low)) * HD ** (-0.5)
    places = jnp.arange(SEQ)
    allowed = (doc_row[:, None] == doc_row[None, :]) & (places[:, None] >= places[None, :])
    scores = jnp.where(allowed, scores, -1e+30)
    highest = lax.optimization_barrier(jnp.max(scores, axis=3, keepdims=True))
    lifted = jnp.exp(scores - highest)
    chances = lifted / lax.optimization_barrier(jnp.sum(lifted, axis=3, keepdims=True))
    attended = both_round(product('ghst,gtd->gshd', low(chances), values_low).reshape(N_TP, SEQ, local_heads * HD))
    out_groups = out_weight.reshape(N_TP, local_heads * HD, D)
    mixed_sum = low_back(lax.optimization_barrier(jnp.sum(low(product('gse,gef->gsf', attended, out_groups)), axis=0)))
    hidden1 = seq_rows + mixed_sum + out_bias
    normed2 = low(layer_norm(hidden1, norm2_gain, norm2_bias))
    copies2 = low_back(jnp.broadcast_to(normed2, (N_TP, SEQ, D)))
    up_groups = up_weight.reshape(D, N_TP, local_units).transpose(1, 0, 2)
    before = low_back(product('gsd,gde->gse', copies2, up_groups) + up_bias.reshape(N_TP, 1, local_units))
    activated = low(jax.nn.gelu(before, approximate=True))
    down_groups = down_weight.reshape(N_TP, local_units, D)
    summed = low_back(lax.optimization_barrier(jnp.sum(low(product('gse,gef->gsf', activated, down_groups)), axis=0)))
    return hidden1 + summed + down_bias

def reference(tokens, doc_ids, norm1_gain, norm1_bias, query_weight, query_bias, keyval_weight, value_bias, out_weight, out_bias, norm2_gain, norm2_bias, up_weight, up_bias, down_weight, down_bias, grad_out):
    params = tuple((weight.astype(jnp.float32) for weight in (norm1_gain, norm1_bias, query_weight, query_bias, keyval_weight, value_bias, out_weight, out_bias, norm2_gain, norm2_bias, up_weight, up_bias, down_weight, down_bias)))
    rows_all = tokens.astype(jnp.float32).reshape(SEQUENCES, SEQ, D)
    cotangents = grad_out.astype(jnp.float32).reshape(SEQUENCES, SEQ, D)

    def accumulate(totals, sequence_item):
        seq_rows, doc_row, cotangent = sequence_item
        result, pullback = jax.vjp(lambda weights, inputs: block_forward(weights, inputs, doc_row), params, seq_rows)
        grad_weights, grad_rows = pullback(cotangent)
        totals = jax.tree.map(lambda current, incoming: current + incoming, totals, grad_weights)
        return (totals, (result.astype(jnp.bfloat16), grad_rows.astype(jnp.bfloat16)))
    initial = jax.tree.map(jnp.zeros_like, params)
    totals, (outputs, grad_rows) = lax.scan(accumulate, initial, (rows_all, doc_ids, cotangents))
    return (outputs.reshape(TOKENS, D), grad_rows.reshape(TOKENS, D), totals[0], totals[1], totals[2], totals[3], totals[4], totals[5], totals[6], totals[7], totals[8], totals[9], totals[10], totals[11], totals[12], totals[13])
```

```python
import functools
import math

import jax
import jax.numpy as jnp
from jax import lax
from jax.experimental import pallas as pl
from jax.experimental.pallas import tpu as pltpu
from jax.sharding import PartitionSpec as P

F32 = jnp.float32
BF16 = jnp.bfloat16
NEG = -1e30
EPS = 1e-05
GELU_A = math.sqrt(2.0 / math.pi)
GELU_B = 0.044715
LOG2E = math.log2(math.e)
VMEM_LIMIT = 56 * 1024 * 1024


def dot_nn(a, b):
    return lax.dot_general(a, b, (((1,), (0,)), ((), ())), preferred_element_type=F32)


def dot_nt(a, b):
    return lax.dot_general(a, b, (((1,), (1,)), ((), ())), preferred_element_type=F32)


def dot_tn(a, b):
    return lax.dot_general(a, b, (((0,), (0,)), ((), ())), preferred_element_type=F32)


def call(kernel, grid, in_specs, out_specs, out_shape, scratch=(), prefetch=0, flops=0, nbytes=0, trans=0, name=None):
    return pl.pallas_call(
        kernel,
        grid_spec=pltpu.PrefetchScalarGridSpec(
            num_scalar_prefetch=prefetch,
            grid=grid,
            in_specs=in_specs,
            out_specs=out_specs,
            scratch_shapes=list(scratch),
        ),
        out_shape=out_shape,
        compiler_params=pltpu.CompilerParams(
            dimension_semantics=("arbitrary",) * len(grid), vmem_limit_bytes=VMEM_LIMIT
        ),
        cost_estimate=pl.CostEstimate(flops=flops, bytes_accessed=nbytes, transcendentals=trans),
        name=name,
    )


def whole(shape):
    return pl.BlockSpec(shape, lambda *_: (0,) * len(shape), pipeline_mode=pl.Buffered(1))


def shape_of(shape, dtype):
    return jax.ShapeDtypeStruct(shape, dtype)


def ln_kernel(x_ref, g_ref, b_ref, o_ref):
    x = x_ref[...].astype(F32)
    c = x - jnp.mean(x, axis=-1, keepdims=True)
    v = jnp.mean(c * c, axis=-1, keepdims=True)
    o_ref[...] = (c * lax.rsqrt(v + EPS) * g_ref[...].astype(F32) + b_ref[...].astype(F32)).astype(BF16)


def layer_norm(x, gain, bias):
    t, d = x.shape
    br = 256
    return call(
        ln_kernel,
        (t // br,),
        [pl.BlockSpec((br, d), lambda i: (i, 0)), whole((1, d)), whole((1, d))],
        pl.BlockSpec((br, d), lambda i: (i, 0)),
        shape_of((t, d), BF16),
        flops=8 * t * d,
        nbytes=4 * t * d,
        name="norm1",
    )(x, gain, bias)


def attn_fwd_kernel(scale, qb, q_ref, k_ref, vt_ref, dcol_ref, drow_ref, o_ref, mask):
    s = q_ref.shape[0]
    reach = s // 2

    def span(j):
        start = max(0, j * qb - reach)
        return start, (j + 1) * qb

    @pl.when(pl.program_id(1) == 0)
    def _():
        for j in range(s // qb):
            lo, hi = span(j)
            kpos = lo + lax.broadcasted_iota(jnp.int32, (hi - lo, qb), 0)
            qpos = j * qb + lax.broadcasted_iota(jnp.int32, (hi - lo, qb), 1)
            ok = (dcol_ref[pl.ds(lo, hi - lo), :] == drow_ref[0, :, pl.ds(j * qb, qb)]) & (kpos <= qpos)
            mask[j, pl.ds(0, hi - lo), :] = jnp.where(ok, 0.0, NEG)

    for j in range(s // qb):
        lo, hi = span(j)
        q = q_ref[pl.ds(j * qb, qb), :]
        sc = dot_nt(k_ref[pl.ds(lo, hi - lo), :], q) + mask[j, pl.ds(0, hi - lo), :]
        top = jnp.max(sc, axis=0, keepdims=True)
        p = jnp.exp2((sc - top) * (scale * LOG2E))
        total = jnp.sum(p, axis=0, keepdims=True)
        o = dot_nn(vt_ref[:, pl.ds(lo, hi - lo)], p.astype(BF16)) / total
        o_ref[pl.ds(j * qb, qb), :] = o.T.astype(BF16)


def attn_fwd(q, k, vt, dcol, drow, seq, hd):
    t, width = q.shape
    heads = width // hd
    qb = 256
    wins = t // seq
    return call(
        functools.partial(attn_fwd_kernel, hd**-0.5, qb),
        (wins, heads),
        [
            pl.BlockSpec((seq, hd), lambda w, h: (w, h)),
            pl.BlockSpec((seq, hd), lambda w, h: (w, 0)),
            pl.BlockSpec((hd, seq), lambda w, h: (0, w)),
            pl.BlockSpec((seq, 1), lambda w, h: (w, 0)),
            pl.BlockSpec((1, 1, seq), lambda w, h: (w, 0, 0)),
        ],
        pl.BlockSpec((seq, hd), lambda w, h: (w, h)),
        shape_of((t, width), BF16),
        scratch=[pltpu.VMEM((seq // qb, seq // 2 + qb, qb), F32)],
        flops=4 * t * seq * width * 5 // 8,
        nbytes=4 * t * width + 4 * t * hd,
        trans=t * seq * heads * 5 // 8,
        name="attn_fwd",
    )(q, k, vt, dcol, drow)


def proj_ln_kernel(att_ref, w_ref, x_ref, ob_ref, g_ref, b_ref, h_ref, n_ref):
    att = att_ref[...]
    mixed = jnp.concatenate([dot_nn(att, w_ref[i]) for i in range(w_ref.shape[0])], axis=1)
    h = x_ref[...].astype(F32) + mixed + ob_ref[...].astype(F32)
    h_ref[...] = h
    c = h - jnp.mean(h, axis=-1, keepdims=True)
    v = jnp.mean(c * c, axis=-1, keepdims=True)
    n_ref[...] = (c * lax.rsqrt(v + EPS) * g_ref[...].astype(F32) + b_ref[...].astype(F32)).astype(BF16)


def proj_ln(att, w, x, out_bias, gain, bias):
    r, width = att.shape
    d = x.shape[1]
    br = min(128, r)
    row = pl.BlockSpec((br, d), lambda i: (i, 0))
    return call(
        proj_ln_kernel,
        (r // br,),
        [pl.BlockSpec((br, width), lambda i: (i, 0)), whole(w.shape), row] + [whole((1, d))] * 3,
        [row, row],
        [shape_of((r, d), F32), shape_of((r, d), BF16)],
        flops=2 * r * width * d,
        nbytes=2 * width * d + 10 * r * d,
        name="proj_ln",
    )(att, w, x, out_bias, gain, bias)


def up_kernel(n_ref, w_ref, b_ref, da_ref, act_ref, gb_ref, gs_ref):
    v = dot_nn(n_ref[...], w_ref[...]) + b_ref[...].astype(F32)
    v2 = v * v
    t = jnp.tanh(GELU_A * v * (1.0 + GELU_B * v2))
    half = 0.5 * (1.0 + t)
    act_ref[...] = (v * half).astype(BF16)
    slope = half + 0.5 * v * (1.0 - t * t) * (GELU_A * (1.0 + 3.0 * GELU_B * v2))
    gb = (da_ref[...].astype(F32) * slope).astype(BF16)
    gb_ref[...] = gb
    gs_ref[...] = jnp.sum(gb.astype(F32), axis=0, keepdims=True)


def ffn_up(n, w, b, da):
    r, d = n.shape
    u = w.shape[1]
    bn = 256
    col = pl.BlockSpec((r, bn), lambda j: (0, j))
    return call(
        up_kernel,
        (u // bn,),
        [whole((r, d)), pl.BlockSpec((d, bn), lambda j: (0, j)), pl.BlockSpec((1, bn), lambda j: (0, j)), col],
        [col, col, pl.BlockSpec((1, bn), lambda j: (0, j))],
        [shape_of((r, u), BF16), shape_of((r, u), BF16), shape_of((1, u), F32)],
        flops=2 * r * d * u,
        nbytes=2 * d * u + 6 * r * u + 2 * r * d,
        trans=r * u,
        name="ffn_up",
    )(n, w, b, da)


def norm2_back_kernel(count, *refs):
    parts = refs[: count]
    h_ref, go_ref, g_ref, w_ref, gh_ref, gm_ref, ga_ref, sums_ref = refs[count:]

    @pl.when(pl.program_id(0) == 0)
    def _():
        sums_ref[...] = jnp.zeros_like(sums_ref)

    gn = parts[0][...].astype(F32)
    for part in parts[1:]:
        gn = gn + part[...].astype(F32)
    h = h_ref[...]
    c = h - jnp.mean(h, axis=-1, keepdims=True)
    inv = lax.rsqrt(jnp.mean(c * c, axis=-1, keepdims=True) + EPS)
    nrm = c * inv
    u = gn * g_ref[...].astype(F32)
    cot = go_ref[...].astype(F32)
    gh = cot + inv * (u - jnp.mean(u, axis=-1, keepdims=True) - nrm * jnp.mean(u * nrm, axis=-1, keepdims=True))
    gh_ref[...] = gh
    gm = gh.astype(BF16)
    gm_ref[...] = gm
    cols = w_ref.shape[2]
    ga = dot_nt(gm[:, :cols], w_ref[0])
    for i in range(1, w_ref.shape[0]):
        ga = ga + dot_nt(gm[:, i * cols : (i + 1) * cols], w_ref[i])
    ga_ref[...] = ga.astype(BF16)
    sums_ref[0:1, :] += jnp.sum(gn * nrm, axis=0, keepdims=True)
    sums_ref[1:2, :] += jnp.sum(gn, axis=0, keepdims=True)
    sums_ref[2:3, :] += jnp.sum(gh, axis=0, keepdims=True)
    sums_ref[3:4, :] += jnp.sum(cot, axis=0, keepdims=True)


def norm2_back(parts, h, go, gain, w):
    r, d = h.shape
    width = w.shape[1]
    br = min(128, r)
    row = pl.BlockSpec((br, d), lambda i: (i, 0))
    wide = pl.BlockSpec((br, width), lambda i: (i, 0))
    return call(
        functools.partial(norm2_back_kernel, len(parts)),
        (r // br,),
        [row] * len(parts) + [row, row, whole((1, d)), whole(w.shape)],
        [row, row, wide, pl.BlockSpec((8, d), lambda i: (0, 0))],
        [shape_of((r, d), F32), shape_of((r, d), BF16), shape_of((r, width), BF16), shape_of((8, d), F32)],
        flops=2 * r * width * d,
        nbytes=2 * width * d + 20 * r * d,
        name="norm2_back",
    )(*parts, h, go, gain, w)


def attn_bwd_kernel(scale, qb, reach, row0_ref, q_ref, go_ref, k_ref, v_ref, kt_ref, dcol_ref, drow_ref, gq_ref, gk_ref, gv_ref, mask):
    rows = q_ref.shape[0]
    span = reach + qb
    first = pl.program_id(0) == 0

    def start(j):
        at = jnp.maximum(row0_ref[0] + j * qb - reach, 0)
        return pl.multiple_of(at, qb)

    @pl.when(first)
    def _():
        gk_ref[...] = jnp.zeros_like(gk_ref)
        gv_ref[...] = jnp.zeros_like(gv_ref)
        for j in range(rows // qb):
            lo = start(j)
            kpos = lo + lax.broadcasted_iota(jnp.int32, (span, qb), 0)
            qpos = row0_ref[0] + j * qb + lax.broadcasted_iota(jnp.int32, (span, qb), 1)
            ok = (dcol_ref[pl.ds(lo, span), :] == drow_ref[:, pl.ds(j * qb, qb)]) & (kpos <= qpos)
            mask[j] = jnp.where(ok, 0.0, NEG)

    for j in range(rows // qb):
        lo = start(j)
        q = q_ref[pl.ds(j * qb, qb), :]
        go = go_ref[pl.ds(j * qb, qb), :]
        k = k_ref[pl.ds(lo, span), :]
        sc = dot_nt(k, q) + mask[j]
        top = jnp.max(sc, axis=0, keepdims=True)
        e = jnp.exp2((sc - top) * (scale * LOG2E))
        p = e * (1.0 / jnp.sum(e, axis=0, keepdims=True))
        dp = dot_nt(v_ref[pl.ds(lo, span), :], go)
        pd = p * dp
        delta = jnp.sum(pd, axis=0, keepdims=True)
        ds = ((pd - p * delta) * scale).astype(BF16)
        gk_ref[pl.ds(lo, span), :] += dot_nn(ds, q)
        gv_ref[pl.ds(lo, span), :] += dot_nn(p.astype(BF16), go)
        gq_ref[pl.ds(j * qb, qb), :] = dot_nn(kt_ref[:, pl.ds(lo, span)], ds).T.astype(BF16)


def attn_bwd(row0, q, go, k, v, kt, dcol, drow, hd):
    r, width = q.shape
    s = k.shape[0]
    heads = width // hd
    qb = min(256, r)
    reach = s // 2
    head = pl.BlockSpec((r, hd), lambda h, *_: (0, h))
    keep = pl.BlockSpec((s, hd), lambda h, *_: (0, 0))
    return call(
        functools.partial(attn_bwd_kernel, hd**-0.5, qb, reach),
        (heads,),
        [head, head, whole((s, hd)), whole((s, hd)), whole((hd, s)), whole((s, 1)), whole((1, r))],
        [head, keep, keep],
        [shape_of((r, width), BF16), shape_of((s, hd), F32), shape_of((s, hd), F32)],
        scratch=[pltpu.VMEM((r // qb, reach + qb, qb), F32)],
        prefetch=1,
        flops=10 * r * (reach + qb) * width,
        nbytes=6 * r * width + 16 * s * hd,
        trans=r * (reach + qb) * heads,
        name="attn_bwd",
    )(row0, q, go, k, v, kt, dcol, drow)


def norm1_back_kernel(gq_ref, gkv_ref, wq_ref, wkv_ref, x_ref, gh_ref, g_ref, gt_ref, sums_ref, small_ref):
    @pl.when(pl.program_id(0) == 0)
    def _():
        sums_ref[...] = jnp.zeros_like(sums_ref)
        small_ref[...] = jnp.zeros_like(small_ref)

    gq = gq_ref[...]
    gkv = gkv_ref[...]
    gn = dot_nt(gq, wq_ref[...]) + dot_nt(gkv, wkv_ref[...])
    x = x_ref[...].astype(F32)
    c = x - jnp.mean(x, axis=-1, keepdims=True)
    inv = lax.rsqrt(jnp.mean(c * c, axis=-1, keepdims=True) + EPS)
    nrm = c * inv
    u = gn * g_ref[...].astype(F32)
    gx = inv * (u - jnp.mean(u, axis=-1, keepdims=True) - nrm * jnp.mean(u * nrm, axis=-1, keepdims=True))
    gt_ref[...] = (gh_ref[...] + gx).astype(BF16)
    sums_ref[0:1, :] += jnp.sum(gn * nrm, axis=0, keepdims=True)
    sums_ref[1:2, :] += jnp.sum(gn, axis=0, keepdims=True)
    sums_ref[2:3, :] += jnp.sum(gq.astype(F32), axis=0, keepdims=True)
    small_ref[0:1, :] += jnp.sum(gkv.astype(F32), axis=0, keepdims=True)


def norm1_back(gq, gkv, wq, wkv, x, gh, gain):
    r, d = x.shape
    br = min(128, r)
    row = pl.BlockSpec((br, d), lambda i: (i, 0))
    kvw = gkv.shape[1]
    return call(
        norm1_back_kernel,
        (r // br,),
        [row, pl.BlockSpec((br, kvw), lambda i: (i, 0)), whole(wq.shape), whole(wkv.shape), row, row, whole((1, d))],
        [row, pl.BlockSpec((8, d), lambda i: (0, 0)), pl.BlockSpec((8, kvw), lambda i: (0, 0))],
        [shape_of((r, d), BF16), shape_of((8, d), F32), shape_of((8, kvw), F32)],
        flops=2 * r * d * (gq.shape[1] + kvw),
        nbytes=2 * d * (gq.shape[1] + kvw) + 12 * r * d,
        name="norm1_back",
    )(gq, gkv, wq, wkv, x, gh, gain)


def stage_orders(bits):
    order = list(range(bits))
    return [order, order[1:] + order[:1]]


def block_at(m, p, order):
    nb = len(order)
    b = 0
    for k, bit in enumerate(order):
        b = b + ((((p >> (nb - 1 - k)) & 1) ^ 1 ^ ((m >> (bit + 1)) & 1)) << bit)
    return b


def grad_kernel(count, keep, m_ref, *refs):
    left, right = refs[:count], refs[count : 2 * count]
    acc = dot_tn(left[0][...], right[0][...])
    for a, b in zip(left[1:], right[1:]):
        acc = acc + dot_tn(a[...], b[...])
    if not keep:
        refs[2 * count][0, 0] = acc.astype(BF16)
        return
    acc = (acc + refs[2 * count][0, 0].astype(F32)).astype(BF16)
    half = pl.program_id(0)
    p = pl.program_id(1)
    places = pl.num_programs(1)
    for h in range(2):
        send_ref, keep_ref = refs[2 * count + 1 + 2 * h], refs[2 * count + 2 + 2 * h]

        @pl.when((half == h) & (p < places // 2))
        def _(send_ref=send_ref):
            send_ref[0] = acc

        @pl.when((half == h) & (p >= places // 2))
        def _(keep_ref=keep_ref):
            keep_ref[0] = acc


def grad_call(m, ndp, lefts, rights, got=None):
    keep = got is not None
    d, n = lefts[0].shape[1], rights[0].shape[1]
    places = ndp // 2
    hp = places // 2
    f = d // ndp
    orders = stage_orders(places.bit_length() - 1)

    def left_map(h, p, m_ref):
        me = m_ref[0]
        b = jnp.where(h == 0, block_at(me, p, orders[0]), block_at(me, p, orders[1]))
        core = me & 1
        return (0, 2 * b + (core if keep else 1 - core))

    specs = [pl.BlockSpec((a.shape[0], f), left_map) for a in lefts]
    specs += [pl.BlockSpec((b.shape[0], n // 2), lambda h, p, *_: (0, h)) for b in rights]
    block = pl.BlockSpec((1, 1, f, n // 2), lambda h, p, *_: (h, p, 0, 0))
    if keep:
        specs.append(block)
        outs, shapes = [], []
        for half in range(2):
            outs.append(
                pl.BlockSpec((1, f, n // 2), lambda h, p, *_, half=half: (jnp.where(h == half, jnp.minimum(p, hp - 1), (h > half) * (hp - 1)), 0, 0))
            )
            outs.append(
                pl.BlockSpec((1, f, n // 2), lambda h, p, *_, half=half: (jnp.where(h == half, jnp.maximum(p - hp, 0), (h > half) * (hp - 1)), 0, 0))
            )
            shapes += [shape_of((hp, f, n // 2), BF16)] * 2
    else:
        outs, shapes = block, shape_of((2, places, f, n // 2), BF16)
    k = sum(a.shape[0] for a in lefts)
    return call(
        functools.partial(grad_kernel, len(lefts), keep),
        (2, places),
        specs,
        outs,
        shapes,
        prefetch=1,
        flops=k * d * n,
        nbytes=2 * k * (d + n) + d * n,
        name="grad_keep" if keep else "grad_send",
    )(m, *lefts, *rights, *((got,) if keep else ()))


def per_device(
    n,
    ndp,
    tokens,
    doc_ids,
    norm1_gain,
    norm1_bias,
    query_weight,
    query_bias,
    keyval_weight,
    value_bias,
    out_weight,
    out_bias,
    norm2_gain,
    norm2_bias,
    up_weight,
    up_bias,
    down_weight,
    down_bias,
    grad_out,
):
    t_all, d = tokens.shape
    wins, seq = doc_ids.shape
    hd = value_bias.shape[0]
    lq = query_weight.shape[1]
    units = up_weight.shape[1]
    group = n // wins
    rows = t_all // n
    ti = lax.axis_index("tp")
    m = lax.axis_index("dp")
    mv = m.reshape(1)
    r = lax.rem(ti, group)
    win = lax.div(ti, group)
    tok = [None]

    def perm(x, to_dp=lambda a: a, to_tp=lambda a: a):
        pairs = [(a * n + b, to_dp(a) * n + to_tp(b)) for a in range(ndp) for b in range(n)]
        return lax.ppermute(x, ("dp", "tp"), pairs)

    def tp_shift(x, s):
        return perm(x, to_tp=lambda b: (b + s) % n)

    def group_shift(x, s):
        return perm(x, to_tp=lambda b: (b // group) * group + (b + s) % group)

    def tp_at(s):
        return lax.rem(ti + (s % n), n)

    def after(x, *marks):
        return lax.optimization_barrier((x,) + marks)[0]

    def seq_in(x):
        return x if tok[0] is None else after(x, tok[0])

    def seq_out(x):
        tok[0] = x[0] if isinstance(x, (tuple, list)) else x
        return x

    def rows_at(x, start, size):
        return lax.dynamic_slice_in_dim(x, start, size, axis=0)

    vec = lambda v: v.reshape(1, -1)
    n1g, n1b, n2g, n2b = vec(norm1_gain), vec(norm1_bias), vec(norm2_gain), vec(norm2_bias)

    def spread(piece, axis):
        size = piece.shape[axis]
        shape = list(piece.shape)
        shape[axis] = n * size
        full = jnp.zeros(shape, piece.dtype)
        for s in range(n):
            got = piece if s == 0 else tp_shift(piece, s)
            at = [0, 0]
            at[axis] = tp_at(-s) * size
            full = lax.dynamic_update_slice(full, got, at)
        return full

    slab = d // ndp
    uslab = units // ndp
    wo_cols = lax.dynamic_slice_in_dim(out_weight, m * slab, slab, axis=1)
    wo_z = spread(wo_cols, 0)
    wo = lax.all_gather(wo_z, "dp", axis=0, tiled=False)

    n1 = seq_out(layer_norm(tokens, n1g, n1b))
    kv = seq_out(jnp.dot(n1, keyval_weight, preferred_element_type=F32))
    keys = kv[:, :hd].astype(BF16)
    values = (kv[:, hd:] + value_bias.astype(F32)).astype(BF16)
    q = seq_out((jnp.dot(seq_in(n1), query_weight, preferred_element_type=F32) + query_bias.astype(F32)).astype(BF16))
    dcol = doc_ids.reshape(t_all, 1)
    att = seq_out(attn_fwd(q, keys, values.T, dcol, doc_ids.reshape(wins, 1, seq), seq, hd))

    up_far, down_far, upb_far = [], [], []
    att_gots = []
    for t in range(1, wins):
        up_far.append(tp_shift(after(rows_at(up_weight, m * slab, slab), wo_z), t * group))
        upb_far.append(tp_shift(vec(up_bias), t * group))
    for s in range(1, n):
        att_gots.append(tp_shift(rows_at(att, tp_at(s) * rows, rows), s))
    for t in range(1, wins):
        down_far.append(tp_shift(after(rows_at(down_weight, m * uslab, uslab), att_gots[n // 2 - 1]), t * group))
    up_far = [lax.all_gather(after(a, wo), "dp", axis=0, tiled=True) for a in up_far]
    down_far = [lax.all_gather(after(b, a), "dp", axis=0, tiled=True) for a, b in zip(up_far, down_far)]

    go = [rows_at(grad_out, (win * group + lax.rem(r + group - s, group)) * rows, rows) for s in range(group)]

    def grad_act(s, w):
        return seq_out(lax.dot_general(seq_in(go[s]), w, (((1,), (1,)), ((), ())), preferred_element_type=F32).astype(BF16))

    das = [[grad_act(s, down_weight)] for s in range(group)]

    att_own = jnp.zeros((rows, n * lq), BF16)
    att_own = lax.dynamic_update_slice(att_own, rows_at(att, ti * rows, rows), (0, ti * lq))
    for s in range(1, n):
        att_own = lax.dynamic_update_slice(att_own, after(att_gots[s - 1], tok[0]), (0, tp_at(-s) * lq))
    x_own = rows_at(tokens, ti * rows, rows)
    h1, n2 = seq_out(proj_ln(att_own, wo, x_own, vec(out_bias), n2g, n2b))

    ns = [n2] + [group_shift(n2, s) for s in range(1, group)]
    wq_z = spread(after(rows_at(query_weight, m * slab, slab), n2), 1)
    wq = lax.all_gather(after(wq_z, *down_far), "dp", axis=0, tiled=True)
    qb_all = jnp.zeros((n * lq,), BF16)
    qb_all = lax.dynamic_update_slice(qb_all, query_bias, (ti * lq,))
    for s in range(1, n):
        qb_all = lax.dynamic_update_slice(qb_all, tp_shift(query_bias, s), (tp_at(-s) * lq,))

    ups = [up_weight] + up_far
    downs = [down_weight] + down_far
    upbs = [vec(up_bias)] + upb_far
    acts = [[None] * wins for _ in range(group)]
    gbs = [[None] * wins for _ in range(group)]
    gsums = [[None] * wins for _ in range(group)]

    def up(s, k):
        acts[s][k], gbs[s][k], gsums[s][k] = seq_out(ffn_up(seq_in(ns[s]), ups[k], upbs[k], das[s][k]))

    def back_up(s):
        out = None
        for k in range(wins):
            part = lax.dot_general(seq_in(gbs[s][k]) if k == 0 else gbs[s][k], ups[k], (((1,), (1,)), ((), ())), preferred_element_type=F32)
            out = part if out is None else out + part
        return seq_out(out.astype(BF16))

    def down(s):
        out = None
        for k in range(wins):
            part = jnp.dot(seq_in(acts[s][k]) if k == 0 else acts[s][k], downs[k], preferred_element_type=F32)
            out = part if out is None else out + part
        return seq_out(out.astype(BF16))

    def grad_send(lefts, rights):
        return perm(seq_out(grad_call(mv, ndp, [seq_in(lefts[0])] + lefts[1:], rights)), to_dp=lambda a: a ^ 1)

    def grad_keep(lefts, rights, got):
        sa, ka, sb, kb = seq_out(grad_call(mv, ndp, [seq_in(lefts[0])] + lefts[1:], rights, got))
        res = []
        for order, send, keep in zip(stage_orders((ndp // 2).bit_length() - 1), (sa, sb), (ka, kb)):
            for b in order:
                x = keep.astype(F32) + perm(send, to_dp=lambda a: a ^ (2 << b)).astype(F32)
                x = x.astype(BF16)
                half = x.shape[0] // 2
                if half:
                    send, keep = x[:half], x[half:]
            res.append(x[0])
        return jnp.concatenate(res, axis=1)

    late = list(range(1, group)) + [0]
    up(0, 0)
    for s in range(1, group):
        up(s, 0)
    act_k = lambda k: [acts[s][k] for s in range(group)]
    gb_k = lambda k: [gbs[s][k] for s in range(group)]
    got_up, got_down, g_up, g_down = {}, {}, {}, {}
    got_up[0] = grad_send(ns, gb_k(0))
    got_down[0] = grad_send(go, act_k(0))
    g_up[0] = grad_keep(ns, gb_k(0), got_up[0])
    g_down[0] = grad_keep(go, act_k(0), got_down[0])
    gn2_parts, sum_parts = [None] * group, [None] * group
    for s in late:
        for k in range(1, wins):
            das[s].append(grad_act(s, downs[k]))
            up(s, k)
        part = back_up(s)
        gn2_parts[s] = part if s == 0 else group_shift(part, -s)
    for s in late:
        part = down(s)
        sum_parts[s] = part if s == 0 else group_shift(after(part, gn2_parts[1]), -s)
    for k in range(1, wins):
        got_up[k] = grad_send(ns, gb_k(k))
        got_down[k] = grad_send(go, act_k(k))
    n1_own = rows_at(n1, ti * rows, rows)
    q_own = seq_out((jnp.dot(seq_in(n1_own), wq, preferred_element_type=F32) + qb_all.astype(F32)).astype(BF16))

    gh1, gm, gatt, sums2 = seq_out(norm2_back(gn2_parts, seq_in(h1), go[0], n2g, wo))
    k_win = rows_at(keys, win * seq, seq)
    v_win = rows_at(values, win * seq, seq)
    row0 = r * rows
    d_win = rows_at(dcol, win * seq, seq)
    d_own = rows_at(dcol, ti * rows, rows).reshape(1, rows)
    gq, gk, gv = seq_out(attn_bwd(row0.reshape(1), q_own, gatt, k_win, v_win, k_win.T, d_win, d_own, hd))
    gkv_part = jnp.concatenate([gk, gv], axis=1)
    gkv = rows_at(gkv_part, row0, rows)
    got_kv = [
        group_shift(rows_at(gkv_part, lax.rem(r + s, group) * rows, rows).astype(BF16), s) for s in range(1, group)
    ]
    for k in range(1, wins):
        g_up[k] = grad_keep(ns, gb_k(k), got_up[k])
    for got in got_kv:
        gkv = gkv + after(got, tok[0]).astype(F32)
    gkv = gkv.astype(BF16)
    gt, sums1, small = seq_out(norm1_back(seq_in(gq), gkv, wq, keyval_weight, x_own, gh1, n1g))
    grad_tokens = lax.all_gather(gt, "tp", axis=0, tiled=True)
    for k in range(1, wins):
        g_down[k] = grad_keep(go, act_k(k), got_down[k])

    total = h1 + down_bias.astype(F32)
    for sp in sum_parts:
        total = total + sp.astype(F32)
    output = lax.all_gather(total.astype(BF16), "tp", axis=0, tiled=True)

    gqkv = jnp.concatenate([gq, gkv], axis=1)
    got_out = grad_send([gm], [att_own])
    got_qkv = grad_send([n1_own], [gqkv])
    g_out = grad_keep([gm], [att_own], got_out)
    g_qkv = grad_keep([n1_own], [gqkv], got_qkv)

    g_upw, g_downw = g_up[0].astype(F32), g_down[0].astype(F32)
    for t in range(1, wins):
        g_upw = g_upw + tp_shift(g_up[t], -t * group).astype(F32)
        g_downw = g_downw + tp_shift(g_down[t], -t * group).astype(F32)

    def tp_scatter(x, cut):
        out = cut(x, ti).astype(F32)
        for s in range(1, n):
            out = out + tp_shift(cut(x, tp_at(s)), s).astype(F32)
        return out

    take_cols = lambda x, i: lax.dynamic_slice_in_dim(x, i * lq, lq, axis=1)
    g_outw = tp_scatter(g_out, take_cols).T
    g_qw = tp_scatter(g_qkv[:, : n * lq], take_cols)
    kv_rows = g_qkv.shape[0] // n
    g_kvw = tp_scatter(g_qkv[:, n * lq :], lambda x, i: rows_at(x, i * kv_rows, kv_rows))

    ub = jnp.zeros((n * units,), F32)
    for k in range(wins):
        part = sum(gsums[s][k] for s in range(group)).reshape(units)
        ub = lax.dynamic_update_slice(ub, part, (tp_at(-k * group) * units,))
    pack = jnp.concatenate(
        [sums2[:4].reshape(-1), sums1[:3].reshape(-1), jnp.pad(small[0, hd:], (0, d - hd)), ub]
    )
    step = 1
    while step < ndp:
        pack = pack + perm(pack, to_dp=lambda a: a ^ step)
        step *= 2
    step = 1
    while step < n:
        pack = pack + perm(pack, to_tp=lambda b: b ^ step)
        step *= 2
    piece = lambda row, at, size: lax.dynamic_slice_in_dim(pack, row * d + at, size)
    vs = d // ndp
    qs = lq // ndp
    us = units // ndp
    bs = hd // (ndp * n)
    return (
        output,
        grad_tokens,
        piece(4, m * vs, vs),
        piece(5, m * vs, vs),
        g_qw,
        piece(6, ti * lq + m * qs, qs),
        g_kvw,
        piece(7, (m * n + ti) * bs, bs),
        g_outw,
        piece(2, m * vs, vs),
        piece(0, m * vs, vs),
        piece(1, m * vs, vs),
        g_upw,
        piece(8, ti * units + m * us, us),
        g_downw.T,
        piece(3, m * vs, vs),
    )


def solution(mesh):
    n = mesh.shape["tp"]
    ndp = mesh.shape["dp"]
    return jax.shard_map(
        functools.partial(per_device, n, ndp),
        mesh=mesh,
        in_specs=(
            P("dp", None),
            P("dp", None),
            P(),
            P(),
            P(None, "tp"),
            P("tp"),
            P(),
            P(),
            P("tp", None),
            P(),
            P(),
            P(),
            P(None, "tp"),
            P("tp"),
            P("tp", None),
            P(),
            P("dp", None),
        ),
        out_specs=(
            P("dp", None),
            P("dp", None),
            P("dp"),
            P("dp"),
            P("dp", "tp"),
            P(("tp", "dp")),
            P(("dp", "tp"), None),
            P(("dp", "tp")),
            P("tp", "dp"),
            P("dp"),
            P("dp"),
            P("dp"),
            P("dp", "tp"),
            P(("tp", "dp")),
            P("tp", "dp"),
            P("dp"),
        ),
        check_vma=False,
    )
```

```python
import functools
import math

import jax
import jax.numpy as jnp
from jax import lax
from jax.experimental import pallas as pl
from jax.experimental.pallas import tpu as pltpu
from jax.sharding import PartitionSpec as P

F32 = jnp.float32
BF16 = jnp.bfloat16
NEG = -1e30
EPS = 1e-05
GELU_A = math.sqrt(2.0 / math.pi)
GELU_B = 0.044715
LOG2E = math.log2(math.e)
VMEM_LIMIT = 56 * 1024 * 1024


def dot_nn(a, b):
    return lax.dot_general(a, b, (((1,), (0,)), ((), ())), preferred_element_type=F32)


def dot_nt(a, b):
    return lax.dot_general(a, b, (((1,), (1,)), ((), ())), preferred_element_type=F32)


def dot_tn(a, b):
    return lax.dot_general(a, b, (((0,), (0,)), ((), ())), preferred_element_type=F32)


def call(kernel, grid, in_specs, out_specs, out_shape, scratch=(), prefetch=0, flops=0, nbytes=0, trans=0, name=None):
    return pl.pallas_call(
        kernel,
        grid_spec=pltpu.PrefetchScalarGridSpec(
            num_scalar_prefetch=prefetch,
            grid=grid,
            in_specs=in_specs,
            out_specs=out_specs,
            scratch_shapes=list(scratch),
        ),
        out_shape=out_shape,
        compiler_params=pltpu.CompilerParams(
            dimension_semantics=("arbitrary",) * len(grid), vmem_limit_bytes=VMEM_LIMIT
        ),
        cost_estimate=pl.CostEstimate(flops=flops, bytes_accessed=nbytes, transcendentals=trans),
        name=name,
    )


def whole(shape):
    return pl.BlockSpec(shape, lambda *_: (0,) * len(shape), pipeline_mode=pl.Buffered(1))


def shape_of(shape, dtype):
    return jax.ShapeDtypeStruct(shape, dtype)


def ln_kernel(win_ref, x_ref, g_ref, b_ref, o_ref):
    x = x_ref[...].astype(F32)
    c = x - jnp.mean(x, axis=-1, keepdims=True)
    v = jnp.mean(c * c, axis=-1, keepdims=True)
    o_ref[...] = (c * lax.rsqrt(v + EPS) * g_ref[...].astype(F32) + b_ref[...].astype(F32)).astype(BF16)


def layer_norm(win, x, gain, bias, t):
    d = x.shape[1]
    br = 256
    return call(
        ln_kernel,
        (t // br,),
        [pl.BlockSpec((br, d), lambda i, win_ref: (win_ref[0] * (t // br) + i, 0)), whole((1, d)), whole((1, d))],
        pl.BlockSpec((br, d), lambda i, *_: (i, 0)),
        shape_of((t, d), BF16),
        prefetch=1,
        flops=8 * t * d,
        nbytes=4 * t * d,
        name="norm1",
    )(win, x, gain, bias)


def attn_fwd_kernel(scale, qb, q_ref, k_ref, vt_ref, dcol_ref, drow_ref, o_ref, mask):
    s = q_ref.shape[0]
    reach = s // 2

    def span(j):
        start = max(0, j * qb - reach)
        return start, (j + 1) * qb

    @pl.when(pl.program_id(1) == 0)
    def _():
        for j in range(s // qb):
            lo, hi = span(j)
            kpos = lo + lax.broadcasted_iota(jnp.int32, (hi - lo, qb), 0)
            qpos = j * qb + lax.broadcasted_iota(jnp.int32, (hi - lo, qb), 1)
            ok = (dcol_ref[pl.ds(lo, hi - lo), :] == drow_ref[0, :, pl.ds(j * qb, qb)]) & (kpos <= qpos)
            mask[j, pl.ds(0, hi - lo), :] = jnp.where(ok, 0.0, NEG)

    for j in range(s // qb):
        lo, hi = span(j)
        q = q_ref[pl.ds(j * qb, qb), :]
        sc = dot_nt(k_ref[pl.ds(lo, hi - lo), :], q) + mask[j, pl.ds(0, hi - lo), :]
        top = jnp.max(sc, axis=0, keepdims=True)
        p = jnp.exp2((sc - top) * (scale * LOG2E))
        total = jnp.sum(p, axis=0, keepdims=True)
        o = dot_nn(vt_ref[:, pl.ds(lo, hi - lo)], p.astype(BF16)) / total
        o_ref[pl.ds(j * qb, qb), :] = o.T.astype(BF16)


def attn_fwd(q, k, vt, dcol, drow, seq, hd):
    t, width = q.shape
    heads = width // hd
    qb = 256
    wins = t // seq
    return call(
        functools.partial(attn_fwd_kernel, hd**-0.5, qb),
        (wins, heads),
        [
            pl.BlockSpec((seq, hd), lambda w, h: (w, h)),
            pl.BlockSpec((seq, hd), lambda w, h: (w, 0)),
            pl.BlockSpec((hd, seq), lambda w, h: (0, w)),
            pl.BlockSpec((seq, 1), lambda w, h: (w, 0)),
            pl.BlockSpec((1, 1, seq), lambda w, h: (w, 0, 0)),
        ],
        pl.BlockSpec((seq, hd), lambda w, h: (w, h)),
        shape_of((t, width), BF16),
        scratch=[pltpu.VMEM((seq // qb, seq // 2 + qb, qb), F32)],
        flops=4 * t * seq * width * 5 // 8,
        nbytes=4 * t * width + 4 * t * hd,
        trans=t * seq * heads * 5 // 8,
        name="attn_fwd",
    )(q, k, vt, dcol, drow)


def proj_ln_kernel(att_ref, w_ref, x_ref, ob_ref, g_ref, b_ref, h_ref, n_ref):
    att = att_ref[...]
    mixed = jnp.concatenate([dot_nn(att, w_ref[i]) for i in range(w_ref.shape[0])], axis=1)
    h = x_ref[...].astype(F32) + mixed + ob_ref[...].astype(F32)
    h_ref[...] = h
    c = h - jnp.mean(h, axis=-1, keepdims=True)
    v = jnp.mean(c * c, axis=-1, keepdims=True)
    n_ref[...] = (c * lax.rsqrt(v + EPS) * g_ref[...].astype(F32) + b_ref[...].astype(F32)).astype(BF16)


def proj_ln(att, w, x, out_bias, gain, bias):
    r, width = att.shape
    d = x.shape[1]
    br = min(256, r)
    row = pl.BlockSpec((br, d), lambda i: (i, 0))
    return call(
        proj_ln_kernel,
        (r // br,),
        [pl.BlockSpec((br, width), lambda i: (i, 0)), whole(w.shape), row] + [whole((1, d))] * 3,
        [row, row],
        [shape_of((r, d), F32), shape_of((r, d), BF16)],
        flops=2 * r * width * d,
        nbytes=2 * width * d + 10 * r * d,
        name="proj_ln",
    )(att, w, x, out_bias, gain, bias)


def gelu_parts(v):
    v2 = v * v
    g = 1.0 / (1.0 + jnp.exp2(v * (-2.0 * GELU_A * LOG2E * (1.0 + GELU_B * v2))))
    return v * g, g + v * (g * (1.0 - g)) * (2.0 * GELU_A * (1.0 + 3.0 * GELU_B * v2))


def up_kernel(ready, n_ref, w_ref, b_ref, *refs):
    r = n_ref.shape[0]
    parts = 2 if ready else 1
    pair_ref, gs_ref = refs[-2:]
    total = None
    for i in range(parts):
        at = pl.ds(i * (r // parts), r // parts)
        v = dot_nn(n_ref[at, :], w_ref[...]) + b_ref[...].astype(F32)
        da = refs[0][at, :].astype(F32) if ready else dot_nt(refs[0][at, :], refs[1][...])
        act, slope = gelu_parts(v)
        pair_ref[0, at, :] = act.astype(BF16)
        gb = (da * slope).astype(BF16)
        pair_ref[1, at, :] = gb
        part = jnp.sum(gb.astype(F32), axis=0, keepdims=True)
        total = part if total is None else total + part
    gs_ref[...] = total


def ffn_up(n, w, b, da=None, go=None, down=None):
    r, d = n.shape
    u = w.shape[1]
    ready = da is not None
    bn = min(512 if ready else 256, u)
    col = pl.BlockSpec((r, bn), lambda j: (0, j))
    line = pl.BlockSpec((1, bn), lambda j: (0, j))
    extra = [col] if ready else [whole((r, d)), pl.BlockSpec((bn, d), lambda j: (j, 0))]
    return call(
        functools.partial(up_kernel, ready),
        (u // bn,),
        [whole((r, d)), pl.BlockSpec((d, bn), lambda j: (0, j)), line] + extra,
        [pl.BlockSpec((2, r, bn), lambda j: (0, 0, j)), line],
        [shape_of((2, r, u), BF16), shape_of((1, u), F32)],
        flops=(2 if ready else 4) * r * d * u,
        nbytes=2 * d * u + 6 * r * u + 2 * r * d,
        trans=r * u,
        name="ffn_up",
    )(n, w, b, *((da,) if ready else (go, down)))


def product_kernel(count, nt, *refs):
    acc = None
    for x, w in zip(refs[:count], refs[count : 2 * count]):
        part = (dot_nt if nt else dot_nn)(x[...], w[...])
        acc = part if acc is None else acc + part
    refs[-1][...] = acc.astype(BF16)


def plane(x, i):
    return pl.BlockSpec((None,) + x.shape[1:], lambda *_: (i, 0, 0), pipeline_mode=pl.Buffered(1))


def product(xs, at, ws, nt):
    r, k = xs[0].shape[1:]
    n = ws[0].shape[0 if nt else 1]
    bn = 512
    wspec = pl.BlockSpec((bn, k), lambda j: (j, 0)) if nt else pl.BlockSpec((k, bn), lambda j: (0, j))
    return call(
        functools.partial(product_kernel, len(xs), nt),
        (n // bn,),
        [plane(x, at) for x in xs] + [wspec] * len(xs),
        pl.BlockSpec((r, bn), lambda j: (0, j)),
        shape_of((r, n), BF16),
        flops=2 * r * k * n * len(xs),
        nbytes=len(xs) * 2 * k * (r + n) + 2 * r * n,
        name="product",
    )(*xs, *ws)


def norm2_back_kernel(count, *refs):
    parts = refs[: count]
    h_ref, go_ref, g_ref, w_ref, gh_ref, gm_ref, ga_ref, sums_ref = refs[count:]

    @pl.when(pl.program_id(0) == 0)
    def _():
        sums_ref[...] = jnp.zeros_like(sums_ref)

    gn = parts[0][...].astype(F32)
    for part in parts[1:]:
        gn = gn + part[...].astype(F32)
    h = h_ref[...]
    c = h - jnp.mean(h, axis=-1, keepdims=True)
    inv = lax.rsqrt(jnp.mean(c * c, axis=-1, keepdims=True) + EPS)
    nrm = c * inv
    u = gn * g_ref[...].astype(F32)
    cot = go_ref[...].astype(F32)
    gh = cot + inv * (u - jnp.mean(u, axis=-1, keepdims=True) - nrm * jnp.mean(u * nrm, axis=-1, keepdims=True))
    gh_ref[...] = gh
    gm = gh.astype(BF16)
    gm_ref[...] = gm
    cols = w_ref.shape[2]
    ga = dot_nt(gm[:, :cols], w_ref[0])
    for i in range(1, w_ref.shape[0]):
        ga = ga + dot_nt(gm[:, i * cols : (i + 1) * cols], w_ref[i])
    ga_ref[...] = ga.astype(BF16)
    sums_ref[0:1, :] += jnp.sum(gn * nrm, axis=0, keepdims=True)
    sums_ref[1:2, :] += jnp.sum(gn, axis=0, keepdims=True)
    sums_ref[2:3, :] += jnp.sum(gh, axis=0, keepdims=True)
    sums_ref[3:4, :] += jnp.sum(cot, axis=0, keepdims=True)


def norm2_back(parts, h, go, gain, w):
    r, d = h.shape
    width = w.shape[1]
    br = min(256, r)
    row = pl.BlockSpec((br, d), lambda i: (i, 0))
    wide = pl.BlockSpec((br, width), lambda i: (i, 0))
    return call(
        functools.partial(norm2_back_kernel, len(parts)),
        (r // br,),
        [row] * len(parts) + [row, row, whole((1, d)), whole(w.shape)],
        [row, row, wide, pl.BlockSpec((8, d), lambda i: (0, 0))],
        [shape_of((r, d), F32), shape_of((r, d), BF16), shape_of((r, width), BF16), shape_of((8, d), F32)],
        flops=2 * r * width * d,
        nbytes=2 * width * d + 20 * r * d,
        name="norm2_back",
    )(*parts, h, go, gain, w)


def attn_bwd_kernel(scale, qb, reach, row0_ref, q_ref, go_ref, k_ref, v_ref, kt_ref, dcol_ref, drow_ref, gq_ref, gk_ref, gv_ref, mask):
    rows = q_ref.shape[0]
    span = reach + qb
    first = pl.program_id(0) == 0

    def start(j):
        at = jnp.maximum(row0_ref[0] + j * qb - reach, 0)
        return pl.multiple_of(at, qb)

    @pl.when(first)
    def _():
        gk_ref[...] = jnp.zeros_like(gk_ref)
        gv_ref[...] = jnp.zeros_like(gv_ref)
        for j in range(rows // qb):
            lo = start(j)
            kpos = lo + lax.broadcasted_iota(jnp.int32, (span, qb), 0)
            qpos = row0_ref[0] + j * qb + lax.broadcasted_iota(jnp.int32, (span, qb), 1)
            ok = (dcol_ref[pl.ds(lo, span), :] == drow_ref[:, pl.ds(j * qb, qb)]) & (kpos <= qpos)
            mask[j] = jnp.where(ok, 0.0, NEG)

    for j in range(rows // qb):
        lo = start(j)
        q = q_ref[pl.ds(j * qb, qb), :]
        go = go_ref[pl.ds(j * qb, qb), :]
        k = k_ref[pl.ds(lo, span), :]
        sc = dot_nt(k, q) + mask[j]
        top = jnp.max(sc, axis=0, keepdims=True)
        e = jnp.exp2((sc - top) * (scale * LOG2E))
        p = e * (1.0 / jnp.sum(e, axis=0, keepdims=True))
        dp = dot_nt(v_ref[pl.ds(lo, span), :], go)
        pd = p * dp
        delta = jnp.sum(pd, axis=0, keepdims=True)
        ds = ((pd - p * delta) * scale).astype(BF16)
        gk_ref[pl.ds(lo, span), :] += dot_nn(ds, q)
        gv_ref[pl.ds(lo, span), :] += dot_nn(p.astype(BF16), go)
        gq_ref[pl.ds(j * qb, qb), :] = dot_nn(kt_ref[:, pl.ds(lo, span)], ds).T.astype(BF16)


def attn_bwd(part, parts, row0, q, go, k, v, kt, dcol, drow, hd):
    r, width = q.shape[0], q.shape[1] // parts
    s = k.shape[0]
    heads = width // hd
    qb = min(256, r)
    reach = s // 2
    head = pl.BlockSpec((r, hd), lambda h, *_: (0, h))
    head_in = pl.BlockSpec((r, hd), lambda h, *_: (0, h + part * heads))
    keep = pl.BlockSpec((s, hd), lambda h, *_: (0, 0))
    return call(
        functools.partial(attn_bwd_kernel, hd**-0.5, qb, reach),
        (heads,),
        [head_in, head_in, whole((s, hd)), whole((s, hd)), whole((hd, s)), whole((s, 1)), whole((1, r))],
        [head, keep, keep],
        [shape_of((r, width), BF16), shape_of((s, hd), F32), shape_of((s, hd), F32)],
        scratch=[pltpu.VMEM((r // qb, reach + qb, qb), F32)],
        prefetch=1,
        flops=10 * r * (reach + qb) * width,
        nbytes=6 * r * width + 16 * s * hd,
        trans=r * (reach + qb) * heads,
        name="attn_bwd",
    )(row0, q, go, k, v, kt, dcol, drow)


def norm1_back_kernel(gq_ref, gkv_ref, wq_ref, wkv_ref, x_ref, gh_ref, g_ref, gt_ref, sums_ref, small_ref):
    @pl.when(pl.program_id(0) == 0)
    def _():
        sums_ref[...] = jnp.zeros_like(sums_ref)
        small_ref[...] = jnp.zeros_like(small_ref)

    gq = gq_ref[...]
    gkv = gkv_ref[...]
    gn = dot_nt(gq, wq_ref[...]) + dot_nt(gkv, wkv_ref[...])
    x = x_ref[...].astype(F32)
    c = x - jnp.mean(x, axis=-1, keepdims=True)
    inv = lax.rsqrt(jnp.mean(c * c, axis=-1, keepdims=True) + EPS)
    nrm = c * inv
    u = gn * g_ref[...].astype(F32)
    gx = inv * (u - jnp.mean(u, axis=-1, keepdims=True) - nrm * jnp.mean(u * nrm, axis=-1, keepdims=True))
    gt_ref[...] = (gh_ref[...] + gx).astype(BF16)
    sums_ref[0:1, :] += jnp.sum(gn * nrm, axis=0, keepdims=True)
    sums_ref[1:2, :] += jnp.sum(gn, axis=0, keepdims=True)
    sums_ref[2:3, :] += jnp.sum(gq.astype(F32), axis=0, keepdims=True)
    small_ref[0:1, :] += jnp.sum(gkv.astype(F32), axis=0, keepdims=True)


def norm1_back(gq, gkv, wq, wkv, x, gh, gain):
    r, d = x.shape
    br = min(256, r)
    row = pl.BlockSpec((br, d), lambda i: (i, 0))
    kvw = gkv.shape[1]
    return call(
        norm1_back_kernel,
        (r // br,),
        [row, pl.BlockSpec((br, kvw), lambda i: (i, 0)), whole(wq.shape), whole(wkv.shape), row, row, whole((1, d))],
        [row, pl.BlockSpec((8, d), lambda i: (0, 0)), pl.BlockSpec((8, kvw), lambda i: (0, 0))],
        [shape_of((r, d), BF16), shape_of((8, d), F32), shape_of((8, kvw), F32)],
        flops=2 * r * d * (gq.shape[1] + kvw),
        nbytes=2 * d * (gq.shape[1] + kvw) + 12 * r * d,
        name="norm1_back",
    )(gq, gkv, wq, wkv, x, gh, gain)


def stage_orders(bits):
    order = list(range(bits))
    return [order, order[1:] + order[:1]]


def place_in(p, bits, order):
    rel = {bit: (p >> (bits - 1 - k)) & 1 for k, bit in enumerate(range(bits))}
    out = 0
    for bit in order:
        out = 2 * out + rel[bit]
    return out


def table(p, values):
    out = values[0]
    for i, v in enumerate(values[1:], 1):
        out = jnp.where(p == i, v, out)
    return out


def grad_kernel(count, pairs, places, m_ref, *refs):
    lefts = [refs[i * count : (i + 1) * count] for i in range(pairs)]
    rights = [refs[(pairs + i) * count : (pairs + i + 1) * count] for i in range(pairs)]
    outs = refs[2 * pairs * count :]
    bits = places.bit_length() - 1
    p = pl.program_id(1)
    cut = rights[0][0].shape[1] // 2

    def run(left, right):
        acc = dot_tn(left[0][...], right[0][...])
        for a, b in zip(left[1:], right[1:]):
            acc = acc + dot_tn(a[...], b[...])
        acc = acc.astype(BF16)
        for h, order in enumerate(stage_orders(bits)):
            sent = [place_in(i, bits, order) < places // 2 for i in range(places)]
            here = table(p, sent)
            send_ref, keep_ref = outs[2 * h], outs[2 * h + 1]
            part = acc[:, h * cut : (h + 1) * cut]

            @pl.when(here)
            def _(send_ref=send_ref, part=part):
                send_ref[0, 0] = part

            @pl.when(jnp.logical_not(here))
            def _(keep_ref=keep_ref, part=part):
                keep_ref[0, 0] = part

    for i in range(pairs):
        pl.when(pl.program_id(0) == i)(functools.partial(run, lefts[i], rights[i]))


def grad_call(m, ndp, lefts, rights):
    pairs, count = len(lefts), len(lefts[0])
    d, n = lefts[0][0].shape[1], rights[0][0][0].shape[2]
    places = ndp // 2
    bits = places.bit_length() - 1
    hp = places // 2
    f = d // ndp

    def left_map(own, i, p, m_ref):
        me = m_ref[0]
        p = jnp.where(i < own, 0, jnp.where(i > own, places - 1, p))
        b = 0
        for k in range(bits):
            b = b + ((((p >> (bits - 1 - k)) & 1) ^ 1 ^ ((me >> (k + 1)) & 1)) << k)
        return (0, 2 * b + (me & 1))

    specs = [pl.BlockSpec((a.shape[0], f), functools.partial(left_map, i)) for i in range(pairs) for a in lefts[i]]
    specs += [plane(b, at) for i in range(pairs) for b, at in rights[i]]
    outs, shapes = [], []
    for order in stage_orders(bits):
        at = [place_in(i, bits, order) for i in range(places)]
        for first in (0, hp):
            seen = [next((a - first for a in at[: i + 1][::-1] if 0 <= a - first < hp), None) for i in range(places)]
            start = next(a for a in seen if a is not None)
            seen = [start if a is None else a for a in seen]
            outs.append(pl.BlockSpec((1, 1, f, n // 2), lambda i, p, *_, seen=seen: (i, table(p, seen), 0, 0)))
            shapes.append(shape_of((pairs, hp, f, n // 2), BF16))
    k = sum(a.shape[0] for a in lefts[0]) * pairs
    return call(
        functools.partial(grad_kernel, count, pairs, places),
        (pairs, places),
        specs,
        outs,
        shapes,
        prefetch=1,
        flops=k * d * n,
        nbytes=k * d + 2 * k * n + pairs * d * n,
        name="weight_grad",
    )(m, *[a for l in lefts for a in l], *[b for r in rights for b, _ in r])


def copy_kernel(x_ref, o_ref):
    o_ref[...] = x_ref[...]


def copied(x):
    t, d = x.shape
    br = 256
    row = pl.BlockSpec((br, d), lambda i: (i, 0))
    return call(copy_kernel, (t // br,), [row], row, shape_of((t, d), x.dtype), nbytes=4 * t * d, name="copied")(x)


def per_device(
    n,
    ndp,
    tokens,
    doc_ids,
    norm1_gain,
    norm1_bias,
    query_weight,
    query_bias,
    keyval_weight,
    value_bias,
    out_weight,
    out_bias,
    norm2_gain,
    norm2_bias,
    up_weight,
    up_bias,
    down_weight,
    down_bias,
    grad_out,
):
    t_all, d = tokens.shape
    wins, seq = doc_ids.shape
    hd = value_bias.shape[0]
    lq = query_weight.shape[1]
    units = up_weight.shape[1]
    group = n // wins
    rows = t_all // n
    ti = lax.axis_index("tp")
    m = lax.axis_index("dp")
    mv = m.reshape(1)
    r = lax.rem(ti, group)
    win = lax.div(ti, group)
    tok = [None]

    def perm(x, to_dp=lambda a: a, to_tp=lambda a: a):
        pairs = [(a * n + b, to_dp(a) * n + to_tp(b)) for a in range(ndp) for b in range(n)]
        return lax.ppermute(x, ("dp", "tp"), pairs)

    def tp_shift(x, s):
        return perm(x, to_tp=lambda b: (b + s) % n)

    def group_shift(x, s):
        return perm(x, to_tp=lambda b: (b // group) * group + (b + s) % group)

    def tp_at(s):
        return lax.rem(ti + (s % n), n)

    def after(x, *marks):
        return lax.optimization_barrier((x,) + marks)[0]

    def seq_in(x):
        return x if tok[0] is None else after(x, tok[0])

    def seq_out(x):
        tok[0] = x[0] if isinstance(x, (tuple, list)) else x
        return x

    def rows_at(x, start, size):
        return lax.dynamic_slice_in_dim(x, start, size, axis=0)

    vec = lambda v: v.reshape(1, -1)
    n1g, n1b, n2g, n2b = vec(norm1_gain), vec(norm1_bias), vec(norm2_gain), vec(norm2_bias)

    def spread(piece, axis):
        size = piece.shape[axis]
        shape = list(piece.shape)
        shape[axis] = n * size
        full = jnp.zeros(shape, piece.dtype)
        for s in range(n):
            got = piece if s == 0 else tp_shift(piece, s)
            at = [0, 0]
            at[axis] = tp_at(-s) * size
            full = lax.dynamic_update_slice(full, got, at)
        return full

    slab = d // ndp
    uslab = units // ndp

    def arrive(x):
        return after(x, tok[0])

    def core_swap(x):
        return perm(x, to_dp=lambda a: a ^ 1)

    def spread_send(piece):
        return [piece] + [tp_shift(piece, s) for s in range(1, n)]

    def spread_place(gots, axis):
        size = gots[0].shape[axis]
        shape = list(gots[0].shape)
        shape[axis] = n * size
        full = jnp.zeros(shape, gots[0].dtype)
        for s in range(n):
            at = [0, 0]
            at[axis] = tp_at(-s) * size
            full = lax.dynamic_update_slice(full, gots[s] if s == 0 else arrive(gots[s]), at)
        return seq_out(full)

    wq_far = [tp_shift(rows_at(query_weight, m * slab, slab), t * group) for t in range(1, wins)]
    qb_far = [tp_shift(query_bias, t * group) for t in range(1, wins)]
    wo_got = spread_send(lax.dynamic_slice_in_dim(out_weight, m * slab, slab, axis=1))
    n1 = seq_out(layer_norm(win.reshape(1), tokens, n1g, n1b, seq))
    kv = seq_out(jnp.dot(n1, keyval_weight, preferred_element_type=F32))
    keys = kv[:, :hd].astype(BF16)
    values = (kv[:, hd:] + value_bias.astype(F32)).astype(BF16)
    values_t = values.T
    dcol = rows_at(doc_ids, win, 1).reshape(seq, 1)
    drow = rows_at(doc_ids, win, 1).reshape(1, 1, seq)
    wq_far = [lax.all_gather(after(a, kv), "dp", axis=0, tiled=True) for a in wq_far]
    go = [rows_at(grad_out, (win * group + lax.rem(r + group - s, group)) * rows, rows) for s in range(group)]
    das = []

    def grad_act(s):
        das.append(seq_out(lax.dot_general(seq_in(go[s]), down_weight, (((1,), (1,)), ((), ())), preferred_element_type=F32).astype(BF16)))

    def heads(w, b):
        q = seq_out((jnp.dot(seq_in(n1), w, preferred_element_type=F32) + b.astype(F32)).astype(BF16))
        att = seq_out(attn_fwd(q, keys, values_t, dcol, drow, seq, hd))
        got = [rows_at(att, r * rows, rows)]
        return got + [group_shift(rows_at(att, lax.rem(r + s, group) * rows, rows), s) for s in range(1, group)]

    att_got = [heads(query_weight, query_bias)]
    wo_z = spread_place(wo_got, 0)
    wo = lax.all_gather(wo_z, "dp", axis=0, tiled=False)
    up_far = [tp_shift(after(rows_at(up_weight, m * slab, slab), wo_z), t * group) for t in range(1, wins)]
    upb_far = [tp_shift(vec(up_bias), t * group) for t in range(1, wins)]
    for w, b in zip(wq_far, qb_far):
        att_got.append(heads(w, b))
    down_far = [tp_shift(arrive(rows_at(down_weight, m * uslab, uslab)), t * group) for t in range(1, wins)]
    att_own = jnp.zeros((rows, n * lq), BF16)
    for t in range(wins):
        if t == wins - 1:
            for s in range(group):
                grad_act(s)
        for s in range(group):
            col = lax.rem(win * group + lax.rem(r + group - s, group) + n - t * group, n) * lq
            att_own = seq_out(lax.dynamic_update_slice(att_own, arrive(att_got[t][s]), (0, col)))
    up_far = [lax.all_gather(after(a, att_own), "dp", axis=0, tiled=True) for a in up_far]
    x_own = rows_at(tokens, ti * rows, rows)
    h1, n2 = seq_out(proj_ln(att_own, wo, x_own, vec(out_bias), n2g, n2b))

    ns = [n2] + [group_shift(n2, s) for s in range(1, group)]
    down_far = [lax.all_gather(after(b, h1), "dp", axis=0, tiled=True) for b in down_far]
    ups, downs = [up_weight] + up_far, [down_weight] + down_far
    upbs = [vec(up_bias)] + upb_far
    units_of = [[None] * wins for _ in range(group)]
    gsums = [[None] * wins for _ in range(group)]

    def up(s, k):
        x = seq_in(ns[s])
        res = ffn_up(x, ups[k], upbs[k], da=das[s]) if k == 0 else ffn_up(x, ups[k], upbs[k], go=go[s], down=downs[k])
        units_of[s][k], gsums[s][k] = seq_out(res)

    def back_up(s):
        return seq_out(product([seq_in(units_of[s][0])] + units_of[s][1:], 1, ups, True))

    def down(s):
        return seq_out(product([seq_in(units_of[s][0])] + units_of[s][1:], 0, downs, False))

    class Grad:
        def __init__(self, lefts, rights):
            self.lefts = [l + [core_swap(arrive(a)) for a in l] for l in lefts]
            self.rights = [[(a[None], 0) for a in x + [core_swap(arrive(a)) for a in x]] for x in rights]

        def keep(self):
            lefts = [[seq_in(self.lefts[0][0])] + self.lefts[0][1:]] + self.lefts[1:]
            res = seq_out(grad_call(mv, ndp, lefts, self.rights))
            self.orders = [list(o) for o in stage_orders((ndp // 2).bit_length() - 1)]
            self.res = res

        def go(self):
            self.halves = [self.leave(h, arrive(self.res[2 * h]), self.res[2 * h + 1]) for h in range(2)]

        def leave(self, h, send, keep):
            b = self.orders[h].pop(0)
            return keep, perm(send, to_dp=lambda a: a ^ (2 << b))

        def stage(self):
            nxt = []
            for h in range(2):
                keep, got = self.halves[h]
                x = seq_out((keep.astype(F32) + arrive(got).astype(F32)).astype(BF16))
                half = x.shape[1] // 2
                nxt.append(self.leave(h, x[:, :half], x[:, half:]) if half else x[:, 0])
            self.halves = nxt

        def finish(self):
            while self.orders[0]:
                self.stage()
            self.stage()
            return jnp.concatenate(self.halves, axis=2)

    go_swapped = [core_swap(after(g, n1)) for g in go]

    late = list(range(1, group)) + [0]
    gn2_parts, sum_parts = [None] * group, [None] * group

    up(0, 0)
    qb_got = [query_bias] + [tp_shift(after(query_bias, n2), s) for s in range(1, n)]
    for s in range(1, group):
        up(s, 0)
    qb_all = jnp.zeros((n * lq,), BF16)
    for s in range(n):
        qb_all = lax.dynamic_update_slice(qb_all, arrive(qb_got[s]), (tp_at(-s) * lq,))
    qb_all = seq_out(qb_all)
    wq_got = spread_send(after(rows_at(query_weight, m * slab, slab), *ns))
    for s in late:
        for k in range(1, wins):
            up(s, k)
        if s == late[0]:
            wq_z = spread_place(wq_got, 1)
            wq = lax.all_gather(wq_z, "dp", axis=0, tiled=True)
        part = back_up(s)
        gn2_parts[s] = part if s == 0 else group_shift(part, -s)
    for s in late:
        part = down(s)
        sum_parts[s] = part if s == 0 else group_shift(after(part, gn2_parts[1]), -s)
    ffn = []

    def ffn_grad(k):
        g = Grad([], [])
        g.lefts = [ns + ns_swapped, go + go_swapped]
        both = [units_of[s][k] for s in range(group)]
        both = both + [core_swap(arrive(a)) for a in both]
        g.rights = [[(a, 1) for a in both], [(a, 0) for a in both]]
        ffn.append(g)

    gh1, gm, gatt, sums2 = seq_out(norm2_back(gn2_parts, seq_in(h1), go[0], n2g, wo))
    n1_own = rows_at(n1, r * rows, rows)
    q_own = seq_out((jnp.dot(seq_in(n1_own), wq, preferred_element_type=F32) + qb_all.astype(F32)).astype(BF16))
    ns_swapped = [core_swap(arrive(x)) for x in ns]
    ub = jnp.zeros((n * units,), F32)
    for k in range(wins):
        part = sum(gsums[s][k] for s in range(group)).reshape(units)
        ub = lax.dynamic_update_slice(ub, part, (tp_at(-k * group) * units,))
    out_g = Grad([[gm]], [[att_own]])
    for k in range(wins):
        ffn_grad(k)
    row0 = r * rows
    d_own = rows_at(dcol, row0, rows).reshape(1, rows)
    keys_t = keys.T

    gq, gk, gv = seq_out(attn_bwd(0, 1, row0.reshape(1), seq_in(q_own), gatt, keys, values, keys_t, dcol, d_own, hd))
    gkv_part = jnp.concatenate([gk, gv], axis=1)
    gkv = rows_at(gkv_part, row0, rows)
    kv_got = [group_shift(rows_at(gkv_part, lax.rem(r + s, group) * rows, rows).astype(BF16), s) for s in range(1, group)]
    total = seq_in(h1) + down_bias.astype(F32)
    for sp in sum_parts:
        total = total + sp.astype(F32)
    total = seq_out(total.astype(BF16))
    output = lax.all_gather(total, "tp", axis=0, tiled=True)
    for got in kv_got:
        gkv = gkv + arrive(got).astype(F32)
    gkv = gkv.astype(BF16)
    gt, sums1, small = seq_out(norm1_back(seq_in(gq), gkv, wq, keyval_weight, x_own, gh1, n1g))
    qkv_g = Grad([[n1_own]], [[jnp.concatenate([gq, gkv], axis=1)]])
    grad_tokens = lax.all_gather(gt, "tp", axis=0, tiled=True)

    pack = jnp.concatenate(
        [sums2[:4].reshape(-1), sums1[:3].reshape(-1), jnp.pad(small[0, hd:], (0, d - hd)), ub]
    )
    swaps = [dict(to_dp=lambda a, s=1 << i: a ^ s) for i in range(ndp.bit_length() - 1)]
    flying = None

    def swap_small():
        nonlocal pack, flying
        if flying is not None:
            pack = seq_out(pack + arrive(flying))
            flying = None
        if swaps:
            flying = perm(pack, **swaps.pop(0))

    swap_small()
    swap_small()
    out_g.keep()
    swap_small()
    for k in range(1, wins):
        ffn[k].keep()
    while swaps:
        swap_small()
    swap_small()
    pack_got = [tp_shift(pack, s) for s in range(1, n)]
    for k in range(1, wins):
        ffn[k].go()
    qkv_g.keep()
    ffn[0].keep()
    for k in range(1, wins):
        ffn[k].stage()
    out_g.go()
    qkv_g.go()
    far = [tp_shift(ffn[k].finish(), -k * group) for k in range(1, wins)]
    ffn[0].go()
    out_g.stage()
    qkv_g.stage()
    g_out = out_g.finish()[0]
    g_qkv = qkv_g.finish()[0]

    take_cols = lambda x, i: lax.dynamic_slice_in_dim(x, i * lq, lq, axis=1)
    kv_rows = g_qkv.shape[0] // n
    fr = g_qkv.shape[0]

    def share(i):
        kv_part = rows_at(g_qkv[:, n * lq :], i * kv_rows, kv_rows)
        return [take_cols(g_out, i), take_cols(g_qkv, i), kv_part.reshape(-1, lq)]

    mine = share(ti)
    shares = [tp_shift(jnp.concatenate(share(tp_at(s)), axis=0), s) for s in range(1, n)]
    output = seq_out(copied(arrive(output)))
    ffn[0].stage()
    f0 = ffn[0].finish()
    g_upw, g_downw = f0[0].astype(F32), f0[1].astype(F32)
    for got in far:
        got = arrive(got).astype(F32)
        g_upw = g_upw + got[0]
        g_downw = g_downw + got[1]
    g_upw = seq_out(g_upw)
    g_downw = seq_out(g_downw.T).T
    g_outw, g_qw, g_kvw = [x.astype(F32) for x in mine]
    for got in shares:
        got = arrive(got).astype(F32)
        g_outw = g_outw + got[:fr]
        g_qw = g_qw + got[fr : 2 * fr]
        g_kvw = g_kvw + got[2 * fr :]
    g_outw = seq_out(g_outw.T)
    g_kvw = g_kvw.reshape(kv_rows, -1)
    grad_tokens = copied(arrive(grad_tokens))
    pack = lax.dynamic_update_slice(jnp.zeros((n, pack.shape[0]), F32), pack[None], (ti, 0))
    for s in range(1, n):
        pack = lax.dynamic_update_slice(pack, pack_got[s - 1][None], (tp_at(-s), 0))
    pack = jnp.sum(pack, axis=0)
    piece = lambda row, at, size: lax.dynamic_slice_in_dim(pack, row * d + at, size)
    vs = d // ndp
    qs = lq // ndp
    us = units // ndp
    bs = hd // (ndp * n)
    return (
        output,
        grad_tokens,
        piece(4, m * vs, vs),
        piece(5, m * vs, vs),
        g_qw,
        piece(6, ti * lq + m * qs, qs),
        g_kvw,
        piece(7, (m * n + ti) * bs, bs),
        g_outw,
        piece(2, m * vs, vs),
        piece(0, m * vs, vs),
        piece(1, m * vs, vs),
        g_upw,
        piece(8, ti * units + m * us, us),
        g_downw.T,
        piece(3, m * vs, vs),
    )


def solution(mesh):
    n = mesh.shape["tp"]
    ndp = mesh.shape["dp"]
    return jax.shard_map(
        functools.partial(per_device, n, ndp),
        mesh=mesh,
        in_specs=(
            P("dp", None),
            P("dp", None),
            P(),
            P(),
            P(None, "tp"),
            P("tp"),
            P(),
            P(),
            P("tp", None),
            P(),
            P(),
            P(),
            P(None, "tp"),
            P("tp"),
            P("tp", None),
            P(),
            P("dp", None),
        ),
        out_specs=(
            P("dp", None),
            P("dp", None),
            P("dp"),
            P("dp"),
            P("dp", "tp"),
            P(("tp", "dp")),
            P(("dp", "tp"), None),
            P(("dp", "tp")),
            P("tp", "dp"),
            P("dp"),
            P("dp"),
            P("dp"),
            P("dp", "tp"),
            P(("tp", "dp")),
            P("tp", "dp"),
            P("dp"),
        ),
        check_vma=False,
    )
```

```python
import functools
import math

import jax
import jax.numpy as jnp
from jax import lax
from jax.experimental import pallas as pl
from jax.experimental.pallas import tpu as pltpu
from jax.sharding import PartitionSpec as P

F32 = jnp.float32
BF16 = jnp.bfloat16
NEG = -1e30
EPS = 1e-05
GELU_A = math.sqrt(2.0 / math.pi)
GELU_B = 0.044715
LOG2E = math.log2(math.e)
VMEM_LIMIT = 56 * 1024 * 1024


def dot_nn(a, b):
    return lax.dot_general(a, b, (((1,), (0,)), ((), ())), preferred_element_type=F32)


def dot_nt(a, b):
    return lax.dot_general(a, b, (((1,), (1,)), ((), ())), preferred_element_type=F32)


def dot_tn(a, b):
    return lax.dot_general(a, b, (((0,), (0,)), ((), ())), preferred_element_type=F32)


def call(kernel, grid, in_specs, out_specs, out_shape, scratch=(), prefetch=0, flops=0, nbytes=0, trans=0, name=None):
    return pl.pallas_call(
        kernel,
        grid_spec=pltpu.PrefetchScalarGridSpec(
            num_scalar_prefetch=prefetch,
            grid=grid,
            in_specs=in_specs,
            out_specs=out_specs,
            scratch_shapes=list(scratch),
        ),
        out_shape=out_shape,
        compiler_params=pltpu.CompilerParams(
            dimension_semantics=("arbitrary",) * len(grid), vmem_limit_bytes=VMEM_LIMIT
        ),
        cost_estimate=pl.CostEstimate(flops=flops, bytes_accessed=nbytes, transcendentals=trans),
        name=name,
    )


def whole(shape):
    return pl.BlockSpec(shape, lambda *_: (0,) * len(shape), pipeline_mode=pl.Buffered(1))


def shape_of(shape, dtype):
    return jax.ShapeDtypeStruct(shape, dtype)


def ln_kernel(win_ref, x_ref, g_ref, b_ref, o_ref):
    x = x_ref[...].astype(F32)
    c = x - jnp.mean(x, axis=-1, keepdims=True)
    v = jnp.mean(c * c, axis=-1, keepdims=True)
    o_ref[...] = (c * lax.rsqrt(v + EPS) * g_ref[...].astype(F32) + b_ref[...].astype(F32)).astype(BF16)


def layer_norm(win, x, gain, bias, t):
    d = x.shape[1]
    br = 256
    return call(
        ln_kernel,
        (t // br,),
        [pl.BlockSpec((br, d), lambda i, win_ref: (win_ref[0] * (t // br) + i, 0)), whole((1, d)), whole((1, d))],
        pl.BlockSpec((br, d), lambda i, *_: (i, 0)),
        shape_of((t, d), BF16),
        prefetch=1,
        flops=8 * t * d,
        nbytes=4 * t * d,
        name="norm1",
    )(win, x, gain, bias)


def attn_fwd_kernel(scale, qb, q_ref, k_ref, vt_ref, dcol_ref, drow_ref, o_ref, mask):
    s = q_ref.shape[0]
    reach = s // 2

    def span(j):
        start = max(0, j * qb - reach)
        return start, (j + 1) * qb

    @pl.when(pl.program_id(1) == 0)
    def _():
        for j in range(s // qb):
            lo, hi = span(j)
            kpos = lo + lax.broadcasted_iota(jnp.int32, (hi - lo, qb), 0)
            qpos = j * qb + lax.broadcasted_iota(jnp.int32, (hi - lo, qb), 1)
            ok = (dcol_ref[pl.ds(lo, hi - lo), :] == drow_ref[0, :, pl.ds(j * qb, qb)]) & (kpos <= qpos)
            mask[j, pl.ds(0, hi - lo), :] = jnp.where(ok, 0.0, NEG)

    for j in range(s // qb):
        lo, hi = span(j)
        q = q_ref[pl.ds(j * qb, qb), :]
        sc = dot_nt(k_ref[pl.ds(lo, hi - lo), :], q) + mask[j, pl.ds(0, hi - lo), :]
        top = jnp.max(sc, axis=0, keepdims=True)
        p = jnp.exp2((sc - top) * (scale * LOG2E))
        total = jnp.sum(p, axis=0, keepdims=True)
        o = dot_nn(vt_ref[:, pl.ds(lo, hi - lo)], p.astype(BF16)) / total
        o_ref[pl.ds(j * qb, qb), :] = o.T.astype(BF16)


def attn_fwd(q, k, vt, dcol, drow, seq, hd):
    t, width = q.shape
    heads = width // hd
    qb = 256
    wins = t // seq
    return call(
        functools.partial(attn_fwd_kernel, hd**-0.5, qb),
        (wins, heads),
        [
            pl.BlockSpec((seq, hd), lambda w, h: (w, h)),
            pl.BlockSpec((seq, hd), lambda w, h: (w, 0)),
            pl.BlockSpec((hd, seq), lambda w, h: (0, w)),
            pl.BlockSpec((seq, 1), lambda w, h: (w, 0)),
            pl.BlockSpec((1, 1, seq), lambda w, h: (w, 0, 0)),
        ],
        pl.BlockSpec((seq, hd), lambda w, h: (w, h)),
        shape_of((t, width), BF16),
        scratch=[pltpu.VMEM((seq // qb, seq // 2 + qb, qb), F32)],
        flops=4 * t * seq * width * 5 // 8,
        nbytes=4 * t * width + 4 * t * hd,
        trans=t * seq * heads * 5 // 8,
        name="attn_fwd",
    )(q, k, vt, dcol, drow)


def proj_ln_kernel(att_ref, w_ref, x_ref, ob_ref, g_ref, b_ref, h_ref, n_ref):
    att = att_ref[...]
    mixed = jnp.concatenate([dot_nn(att, w_ref[i]) for i in range(w_ref.shape[0])], axis=1)
    h = x_ref[...].astype(F32) + mixed + ob_ref[...].astype(F32)
    h_ref[...] = h
    c = h - jnp.mean(h, axis=-1, keepdims=True)
    v = jnp.mean(c * c, axis=-1, keepdims=True)
    n_ref[...] = (c * lax.rsqrt(v + EPS) * g_ref[...].astype(F32) + b_ref[...].astype(F32)).astype(BF16)


def proj_ln(att, w, x, out_bias, gain, bias):
    r, width = att.shape
    d = x.shape[1]
    br = min(256, r)
    row = pl.BlockSpec((br, d), lambda i: (i, 0))
    return call(
        proj_ln_kernel,
        (r // br,),
        [pl.BlockSpec((br, width), lambda i: (i, 0)), whole(w.shape), row] + [whole((1, d))] * 3,
        [row, row],
        [shape_of((r, d), F32), shape_of((r, d), BF16)],
        flops=2 * r * width * d,
        nbytes=2 * width * d + 10 * r * d,
        name="proj_ln",
    )(att, w, x, out_bias, gain, bias)


def gelu_parts(v):
    v2 = v * v
    g = 1.0 / (1.0 + jnp.exp2(v * (-2.0 * GELU_A * LOG2E * (1.0 + GELU_B * v2))))
    return v * g, g + v * (g * (1.0 - g)) * (2.0 * GELU_A * (1.0 + 3.0 * GELU_B * v2))


def up_kernel(ready, n_ref, w_ref, b_ref, *refs):
    r = n_ref.shape[0]
    parts = 2 if ready else 1
    pair_ref, gs_ref = refs[-2:]
    total = None
    for i in range(parts):
        at = pl.ds(i * (r // parts), r // parts)
        v = dot_nn(n_ref[at, :], w_ref[...]) + b_ref[...].astype(F32)
        da = refs[0][at, :].astype(F32) if ready else dot_nt(refs[0][at, :], refs[1][...])
        act, slope = gelu_parts(v)
        pair_ref[0, at, :] = act.astype(BF16)
        gb = (da * slope).astype(BF16)
        pair_ref[1, at, :] = gb
        part = jnp.sum(gb.astype(F32), axis=0, keepdims=True)
        total = part if total is None else total + part
    gs_ref[...] = total


def ffn_up(n, w, b, da=None, go=None, down=None):
    r, d = n.shape
    u = w.shape[1]
    ready = da is not None
    bn = min(512 if ready else 256, u)
    col = pl.BlockSpec((r, bn), lambda j: (0, j))
    line = pl.BlockSpec((1, bn), lambda j: (0, j))
    extra = [col] if ready else [whole((r, d)), pl.BlockSpec((bn, d), lambda j: (j, 0))]
    return call(
        functools.partial(up_kernel, ready),
        (u // bn,),
        [whole((r, d)), pl.BlockSpec((d, bn), lambda j: (0, j)), line] + extra,
        [pl.BlockSpec((2, r, bn), lambda j: (0, 0, j)), line],
        [shape_of((2, r, u), BF16), shape_of((1, u), F32)],
        flops=(2 if ready else 4) * r * d * u,
        nbytes=2 * d * u + 6 * r * u + 2 * r * d,
        trans=r * u,
        name="ffn_up",
    )(n, w, b, *((da,) if ready else (go, down)))


def product_kernel(count, nt, *refs):
    acc = None
    for x, w in zip(refs[:count], refs[count : 2 * count]):
        part = (dot_nt if nt else dot_nn)(x[...], w[...])
        acc = part if acc is None else acc + part
    refs[-1][...] = acc.astype(BF16)


def plane(x, i):
    return pl.BlockSpec((None,) + x.shape[1:], lambda *_: (i, 0, 0), pipeline_mode=pl.Buffered(1))


def product(xs, at, ws, nt):
    r, k = xs[0].shape[1:]
    n = ws[0].shape[0 if nt else 1]
    bn = 512
    wspec = pl.BlockSpec((bn, k), lambda j: (j, 0)) if nt else pl.BlockSpec((k, bn), lambda j: (0, j))
    return call(
        functools.partial(product_kernel, len(xs), nt),
        (n // bn,),
        [plane(x, at) for x in xs] + [wspec] * len(xs),
        pl.BlockSpec((r, bn), lambda j: (0, j)),
        shape_of((r, n), BF16),
        flops=2 * r * k * n * len(xs),
        nbytes=len(xs) * 2 * k * (r + n) + 2 * r * n,
        name="product",
    )(*xs, *ws)


def norm2_back_kernel(count, *refs):
    parts = refs[: count]
    h_ref, go_ref, g_ref, w_ref, gh_ref, gm_ref, ga_ref, sums_ref = refs[count:]

    @pl.when(pl.program_id(0) == 0)
    def _():
        sums_ref[...] = jnp.zeros_like(sums_ref)

    gn = parts[0][...].astype(F32)
    for part in parts[1:]:
        gn = gn + part[...].astype(F32)
    h = h_ref[...]
    c = h - jnp.mean(h, axis=-1, keepdims=True)
    inv = lax.rsqrt(jnp.mean(c * c, axis=-1, keepdims=True) + EPS)
    nrm = c * inv
    u = gn * g_ref[...].astype(F32)
    cot = go_ref[...].astype(F32)
    gh = cot + inv * (u - jnp.mean(u, axis=-1, keepdims=True) - nrm * jnp.mean(u * nrm, axis=-1, keepdims=True))
    gh_ref[...] = gh
    gm = gh.astype(BF16)
    gm_ref[...] = gm
    cols = w_ref.shape[2]
    ga = dot_nt(gm[:, :cols], w_ref[0])
    for i in range(1, w_ref.shape[0]):
        ga = ga + dot_nt(gm[:, i * cols : (i + 1) * cols], w_ref[i])
    ga_ref[...] = ga.astype(BF16)
    sums_ref[0:1, :] += jnp.sum(gn * nrm, axis=0, keepdims=True)
    sums_ref[1:2, :] += jnp.sum(gn, axis=0, keepdims=True)
    sums_ref[2:3, :] += jnp.sum(gh, axis=0, keepdims=True)
    sums_ref[3:4, :] += jnp.sum(cot, axis=0, keepdims=True)


def norm2_back(parts, h, go, gain, w):
    r, d = h.shape
    width = w.shape[1]
    br = min(256, r)
    row = pl.BlockSpec((br, d), lambda i: (i, 0))
    wide = pl.BlockSpec((br, width), lambda i: (i, 0))
    return call(
        functools.partial(norm2_back_kernel, len(parts)),
        (r // br,),
        [row] * len(parts) + [row, row, whole((1, d)), whole(w.shape)],
        [row, row, wide, pl.BlockSpec((8, d), lambda i: (0, 0))],
        [shape_of((r, d), F32), shape_of((r, d), BF16), shape_of((r, width), BF16), shape_of((8, d), F32)],
        flops=2 * r * width * d,
        nbytes=2 * width * d + 20 * r * d,
        name="norm2_back",
    )(*parts, h, go, gain, w)


def attn_bwd_kernel(scale, qb, reach, row0_ref, q_ref, go_ref, k_ref, v_ref, kt_ref, dcol_ref, drow_ref, gq_ref, gk_ref, gv_ref, mask):
    rows = q_ref.shape[0]
    span = reach + qb
    first = pl.program_id(0) == 0

    def start(j):
        at = jnp.maximum(row0_ref[0] + j * qb - reach, 0)
        return pl.multiple_of(at, qb)

    @pl.when(first)
    def _():
        gk_ref[...] = jnp.zeros_like(gk_ref)
        gv_ref[...] = jnp.zeros_like(gv_ref)
        for j in range(rows // qb):
            lo = start(j)
            kpos = lo + lax.broadcasted_iota(jnp.int32, (span, qb), 0)
            qpos = row0_ref[0] + j * qb + lax.broadcasted_iota(jnp.int32, (span, qb), 1)
            ok = (dcol_ref[pl.ds(lo, span), :] == drow_ref[:, pl.ds(j * qb, qb)]) & (kpos <= qpos)
            mask[j] = jnp.where(ok, 0.0, NEG)

    for j in range(rows // qb):
        lo = start(j)
        q = q_ref[pl.ds(j * qb, qb), :]
        go = go_ref[pl.ds(j * qb, qb), :]
        k = k_ref[pl.ds(lo, span), :]
        sc = dot_nt(k, q) + mask[j]
        top = jnp.max(sc, axis=0, keepdims=True)
        e = jnp.exp2((sc - top) * (scale * LOG2E))
        p = e * (1.0 / jnp.sum(e, axis=0, keepdims=True))
        dp = dot_nt(v_ref[pl.ds(lo, span), :], go)
        pd = p * dp
        delta = jnp.sum(pd, axis=0, keepdims=True)
        ds = ((pd - p * delta) * scale).astype(BF16)
        gk_ref[pl.ds(lo, span), :] += dot_nn(ds, q)
        gv_ref[pl.ds(lo, span), :] += dot_nn(p.astype(BF16), go)
        gq_ref[pl.ds(j * qb, qb), :] = dot_nn(kt_ref[:, pl.ds(lo, span)], ds).T.astype(BF16)


def attn_bwd(part, parts, row0, q, go, k, v, kt, dcol, drow, hd):
    r, width = q.shape[0], q.shape[1] // parts
    s = k.shape[0]
    heads = width // hd
    qb = min(256, r)
    reach = s // 2
    head = pl.BlockSpec((r, hd), lambda h, *_: (0, h))
    head_in = pl.BlockSpec((r, hd), lambda h, *_: (0, h + part * heads))
    keep = pl.BlockSpec((s, hd), lambda h, *_: (0, 0))
    return call(
        functools.partial(attn_bwd_kernel, hd**-0.5, qb, reach),
        (heads,),
        [head_in, head_in, whole((s, hd)), whole((s, hd)), whole((hd, s)), whole((s, 1)), whole((1, r))],
        [head, keep, keep],
        [shape_of((r, width), BF16), shape_of((s, hd), F32), shape_of((s, hd), F32)],
        scratch=[pltpu.VMEM((r // qb, reach + qb, qb), F32)],
        prefetch=1,
        flops=10 * r * (reach + qb) * width,
        nbytes=6 * r * width + 16 * s * hd,
        trans=r * (reach + qb) * heads,
        name="attn_bwd",
    )(row0, q, go, k, v, kt, dcol, drow)


def norm1_back_kernel(gq_ref, gkv_ref, wq_ref, wkv_ref, x_ref, gh_ref, g_ref, gt_ref, sums_ref, small_ref):
    @pl.when(pl.program_id(0) == 0)
    def _():
        sums_ref[...] = jnp.zeros_like(sums_ref)
        small_ref[...] = jnp.zeros_like(small_ref)

    gq = gq_ref[...]
    gkv = gkv_ref[...]
    gn = dot_nt(gq, wq_ref[...]) + dot_nt(gkv, wkv_ref[...])
    x = x_ref[...].astype(F32)
    c = x - jnp.mean(x, axis=-1, keepdims=True)
    inv = lax.rsqrt(jnp.mean(c * c, axis=-1, keepdims=True) + EPS)
    nrm = c * inv
    u = gn * g_ref[...].astype(F32)
    gx = inv * (u - jnp.mean(u, axis=-1, keepdims=True) - nrm * jnp.mean(u * nrm, axis=-1, keepdims=True))
    gt_ref[...] = (gh_ref[...] + gx).astype(BF16)
    sums_ref[0:1, :] += jnp.sum(gn * nrm, axis=0, keepdims=True)
    sums_ref[1:2, :] += jnp.sum(gn, axis=0, keepdims=True)
    sums_ref[2:3, :] += jnp.sum(gq.astype(F32), axis=0, keepdims=True)
    small_ref[0:1, :] += jnp.sum(gkv.astype(F32), axis=0, keepdims=True)


def norm1_back(gq, gkv, wq, wkv, x, gh, gain):
    r, d = x.shape
    br = min(256, r)
    row = pl.BlockSpec((br, d), lambda i: (i, 0))
    kvw = gkv.shape[1]
    return call(
        norm1_back_kernel,
        (r // br,),
        [row, pl.BlockSpec((br, kvw), lambda i: (i, 0)), whole(wq.shape), whole(wkv.shape), row, row, whole((1, d))],
        [row, pl.BlockSpec((8, d), lambda i: (0, 0)), pl.BlockSpec((8, kvw), lambda i: (0, 0))],
        [shape_of((r, d), BF16), shape_of((8, d), F32), shape_of((8, kvw), F32)],
        flops=2 * r * d * (gq.shape[1] + kvw),
        nbytes=2 * d * (gq.shape[1] + kvw) + 12 * r * d,
        name="norm1_back",
    )(gq, gkv, wq, wkv, x, gh, gain)


def stage_orders(bits):
    order = list(range(bits))
    return [order, order[1:] + order[:1]]


def place_in(p, bits, order):
    rel = {bit: (p >> (bits - 1 - k)) & 1 for k, bit in enumerate(range(bits))}
    out = 0
    for bit in order:
        out = 2 * out + rel[bit]
    return out


def table(p, values):
    out = values[0]
    for i, v in enumerate(values[1:], 1):
        out = jnp.where(p == i, v, out)
    return out


def grad_kernel(count, pairs, places, m_ref, *refs):
    lefts = [refs[i * count : (i + 1) * count] for i in range(pairs)]
    rights = [refs[(pairs + i) * count : (pairs + i + 1) * count] for i in range(pairs)]
    outs = refs[2 * pairs * count :]
    bits = places.bit_length() - 1
    p = pl.program_id(1)
    cut = rights[0][0].shape[1] // 2

    def run(left, right):
        acc = dot_tn(left[0][...], right[0][...])
        for a, b in zip(left[1:], right[1:]):
            acc = acc + dot_tn(a[...], b[...])
        acc = acc.astype(BF16)
        for h, order in enumerate(stage_orders(bits)):
            sent = [place_in(i, bits, order) < places // 2 for i in range(places)]
            here = table(p, sent)
            send_ref, keep_ref = outs[2 * h], outs[2 * h + 1]
            part = acc[:, h * cut : (h + 1) * cut]

            @pl.when(here)
            def _(send_ref=send_ref, part=part):
                send_ref[0, 0] = part

            @pl.when(jnp.logical_not(here))
            def _(keep_ref=keep_ref, part=part):
                keep_ref[0, 0] = part

    for i in range(pairs):
        pl.when(pl.program_id(0) == i)(functools.partial(run, lefts[i], rights[i]))


def grad_call(m, ndp, lefts, rights):
    pairs, count = len(lefts), len(lefts[0])
    d, n = lefts[0][0].shape[1], rights[0][0][0].shape[2]
    places = ndp // 2
    bits = places.bit_length() - 1
    hp = places // 2
    f = d // ndp

    def left_map(own, i, p, m_ref):
        me = m_ref[0]
        p = jnp.where(i < own, 0, jnp.where(i > own, places - 1, p))
        b = 0
        for k in range(bits):
            b = b + ((((p >> (bits - 1 - k)) & 1) ^ 1 ^ ((me >> (k + 1)) & 1)) << k)
        return (0, 2 * b + (me & 1))

    specs = [pl.BlockSpec((a.shape[0], f), functools.partial(left_map, i)) for i in range(pairs) for a in lefts[i]]
    specs += [plane(b, at) for i in range(pairs) for b, at in rights[i]]
    outs, shapes = [], []
    for order in stage_orders(bits):
        at = [place_in(i, bits, order) for i in range(places)]
        for first in (0, hp):
            seen = [next((a - first for a in at[: i + 1][::-1] if 0 <= a - first < hp), None) for i in range(places)]
            start = next(a for a in seen if a is not None)
            seen = [start if a is None else a for a in seen]
            outs.append(pl.BlockSpec((1, 1, f, n // 2), lambda i, p, *_, seen=seen: (i, table(p, seen), 0, 0)))
            shapes.append(shape_of((pairs, hp, f, n // 2), BF16))
    k = sum(a.shape[0] for a in lefts[0]) * pairs
    return call(
        functools.partial(grad_kernel, count, pairs, places),
        (pairs, places),
        specs,
        outs,
        shapes,
        prefetch=1,
        flops=k * d * n,
        nbytes=k * d + 2 * k * n + pairs * d * n,
        name="weight_grad",
    )(m, *[a for l in lefts for a in l], *[b for r in rights for b, _ in r])


def copy_kernel(x_ref, o_ref):
    o_ref[...] = x_ref[...]


def copied(x):
    t, d = x.shape
    br = 256
    row = pl.BlockSpec((br, d), lambda i: (i, 0))
    return call(copy_kernel, (t // br,), [row], row, shape_of((t, d), x.dtype), nbytes=4 * t * d, name="copied")(x)


def per_device(
    n,
    ndp,
    tokens,
    doc_ids,
    norm1_gain,
    norm1_bias,
    query_weight,
    query_bias,
    keyval_weight,
    value_bias,
    out_weight,
    out_bias,
    norm2_gain,
    norm2_bias,
    up_weight,
    up_bias,
    down_weight,
    down_bias,
    grad_out,
):
    t_all, d = tokens.shape
    wins, seq = doc_ids.shape
    hd = value_bias.shape[0]
    lq = query_weight.shape[1]
    units = up_weight.shape[1]
    group = n // wins
    rows = t_all // n
    ti = lax.axis_index("tp")
    m = lax.axis_index("dp")
    mv = m.reshape(1)
    r = lax.rem(ti, group)
    win = lax.div(ti, group)
    tok = [None]

    def perm(x, to_dp=lambda a: a, to_tp=lambda a: a):
        pairs = [(a * n + b, to_dp(a) * n + to_tp(b)) for a in range(ndp) for b in range(n)]
        return lax.ppermute(x, ("dp", "tp"), pairs)

    def tp_shift(x, s):
        return perm(x, to_tp=lambda b: (b + s) % n)

    def group_shift(x, s):
        return perm(x, to_tp=lambda b: (b // group) * group + (b + s) % group)

    def tp_at(s):
        return lax.rem(ti + (s % n), n)

    def after(x, *marks):
        return lax.optimization_barrier((x,) + marks)[0]

    def seq_in(x):
        return x if tok[0] is None else after(x, tok[0])

    def seq_out(x):
        tok[0] = x[0] if isinstance(x, (tuple, list)) else x
        return x

    def rows_at(x, start, size):
        return lax.dynamic_slice_in_dim(x, start, size, axis=0)

    vec = lambda v: v.reshape(1, -1)
    n1g, n1b, n2g, n2b = vec(norm1_gain), vec(norm1_bias), vec(norm2_gain), vec(norm2_bias)

    def spread(piece, axis):
        size = piece.shape[axis]
        shape = list(piece.shape)
        shape[axis] = n * size
        full = jnp.zeros(shape, piece.dtype)
        for s in range(n):
            got = piece if s == 0 else tp_shift(piece, s)
            at = [0, 0]
            at[axis] = tp_at(-s) * size
            full = lax.dynamic_update_slice(full, got, at)
        return full

    slab = d // ndp
    uslab = units // ndp

    def arrive(x):
        return after(x, tok[0])

    def core_swap(x):
        return perm(x, to_dp=lambda a: a ^ 1)

    def spread_send(piece):
        return [piece] + [tp_shift(piece, s) for s in range(1, n)]

    def spread_place(gots, axis):
        size = gots[0].shape[axis]
        shape = list(gots[0].shape)
        shape[axis] = n * size
        full = jnp.zeros(shape, gots[0].dtype)
        for s in range(n):
            at = [0, 0]
            at[axis] = tp_at(-s) * size
            full = lax.dynamic_update_slice(full, gots[s] if s == 0 else arrive(gots[s]), at)
        return seq_out(full)

    def with_bias(piece, bias):
        return jnp.concatenate([piece, jnp.broadcast_to(bias.reshape(1, -1), (16, bias.shape[0]))], axis=0)

    wq_slab = with_bias(rows_at(query_weight, m * slab, slab), query_bias)
    wq_far = [tp_shift(wq_slab, t * group) for t in range(1, wins)]
    qb_far = [a[slab] for a in wq_far]
    wo_got = spread_send(lax.dynamic_slice_in_dim(out_weight, m * slab, slab, axis=1))
    n1 = seq_out(layer_norm(win.reshape(1), tokens, n1g, n1b, seq))
    kv = seq_out(jnp.dot(n1, keyval_weight, preferred_element_type=F32))
    keys = kv[:, :hd].astype(BF16)
    values = (kv[:, hd:] + value_bias.astype(F32)).astype(BF16)
    values_t = values.T
    dcol = rows_at(doc_ids, win, 1).reshape(seq, 1)
    drow = rows_at(doc_ids, win, 1).reshape(1, 1, seq)
    wq_far = [lax.all_gather(after(a[:slab], kv), "dp", axis=0, tiled=True) for a in wq_far]
    go = [rows_at(grad_out, (win * group + lax.rem(r + group - s, group)) * rows, rows) for s in range(group)]
    das = []

    def grad_act(s):
        das.append(seq_out(lax.dot_general(seq_in(go[s]), down_weight, (((1,), (1,)), ((), ())), preferred_element_type=F32).astype(BF16)))

    def heads(w, b):
        q = seq_out((jnp.dot(seq_in(n1), w, preferred_element_type=F32) + b.astype(F32)).astype(BF16))
        att = seq_out(attn_fwd(q, keys, values_t, dcol, drow, seq, hd))
        got = [rows_at(att, r * rows, rows)]
        return got + [group_shift(rows_at(att, lax.rem(r + s, group) * rows, rows), s) for s in range(1, group)]

    up_slab = with_bias(rows_at(up_weight, m * slab, slab), up_bias)
    up_far = [tp_shift(after(up_slab, kv), t * group) for t in range(1, wins)]
    att_got = [heads(query_weight, query_bias)]
    wo_z = spread_place(wo_got, 0)
    wo = lax.all_gather(wo_z, "dp", axis=0, tiled=False)
    down_far = [tp_shift(after(rows_at(down_weight, m * uslab, uslab), wo_z), t * group) for t in range(1, wins)]
    for w, b in zip(wq_far, qb_far):
        att_got.append(heads(w, b))
    upb_far = [a[slab : slab + 1] for a in up_far]
    up_far = [lax.all_gather(arrive(a)[:slab], "dp", axis=0, tiled=True) for a in up_far]
    att_own = jnp.zeros((rows, n * lq), BF16)
    for t in range(wins):
        if t == wins - 1:
            for s in range(group):
                grad_act(s)
        for s in range(group):
            col = lax.rem(win * group + lax.rem(r + group - s, group) + n - t * group, n) * lq
            att_own = seq_out(lax.dynamic_update_slice(att_own, arrive(att_got[t][s]), (0, col)))
    x_own = rows_at(tokens, ti * rows, rows)
    h1, n2 = seq_out(proj_ln(att_own, wo, x_own, vec(out_bias), n2g, n2b))

    ns = [n2] + [group_shift(n2, s) for s in range(1, group)]
    down_far = [lax.all_gather(after(b, h1), "dp", axis=0, tiled=True) for b in down_far]
    ups, downs = [up_weight] + up_far, [down_weight] + down_far
    upbs = [vec(up_bias)] + upb_far
    units_of = [[None] * wins for _ in range(group)]
    gsums = [[None] * wins for _ in range(group)]

    def up(s, k):
        x = seq_in(ns[s])
        res = ffn_up(x, ups[k], upbs[k], da=das[s]) if k == 0 else ffn_up(x, ups[k], upbs[k], go=go[s], down=downs[k])
        units_of[s][k], gsums[s][k] = seq_out(res)

    def back_up(s):
        return seq_out(product([seq_in(units_of[s][0])] + units_of[s][1:], 1, ups, True))

    def down(s):
        return seq_out(product([seq_in(units_of[s][0])] + units_of[s][1:], 0, downs, False))

    class Grad:
        def __init__(self, lefts, rights):
            self.lefts = [l + [core_swap(arrive(a)) for a in l] for l in lefts]
            self.rights = [[(a[None], 0) for a in x + [core_swap(arrive(a)) for a in x]] for x in rights]

        def keep(self):
            lefts = [[seq_in(self.lefts[0][0])] + self.lefts[0][1:]] + self.lefts[1:]
            res = seq_out(grad_call(mv, ndp, lefts, self.rights))
            self.orders = [list(o) for o in stage_orders((ndp // 2).bit_length() - 1)]
            self.res = res

        def go(self):
            self.halves = [self.leave(h, arrive(self.res[2 * h]), self.res[2 * h + 1]) for h in range(2)]

        def leave(self, h, send, keep):
            b = self.orders[h].pop(0)
            return keep, perm(send, to_dp=lambda a: a ^ (2 << b))

        def stage(self):
            nxt = []
            for h in range(2):
                keep, got = self.halves[h]
                x = seq_out((keep.astype(F32) + arrive(got).astype(F32)).astype(BF16))
                half = x.shape[1] // 2
                nxt.append(self.leave(h, x[:, :half], x[:, half:]) if half else x[:, 0])
            self.halves = nxt

        def finish(self):
            while self.orders[0]:
                self.stage()
            self.stage()
            return jnp.concatenate(self.halves, axis=2)

    go_swapped = [core_swap(after(g, n1)) for g in go]

    late = list(range(1, group)) + [0]
    gn2_parts, sum_parts = [None] * group, [None] * group

    up(0, 0)
    for s in range(1, group):
        up(s, 0)
    wq_got = spread_send(after(wq_slab, *ns))
    for s in late:
        for k in range(1, wins):
            up(s, k)
        if s == late[0]:
            wq_z = spread_place(wq_got, 1)
            qb_all = wq_z[slab]
            wq = lax.all_gather(wq_z[:slab], "dp", axis=0, tiled=True)
        part = back_up(s)
        gn2_parts[s] = part if s == 0 else group_shift(part, -s)
    for s in late:
        part = down(s)
        sum_parts[s] = part if s == 0 else group_shift(part, -s)
    ffn = []

    def ffn_grad(k):
        g = Grad([], [])
        g.lefts = [ns + ns_swapped, go + go_swapped]
        both = [units_of[s][k] for s in range(group)]
        both = both + [core_swap(arrive(a)) for a in both]
        g.rights = [[(a, 1) for a in both], [(a, 0) for a in both]]
        ffn.append(g)

    gh1, gm, gatt, sums2 = seq_out(norm2_back(gn2_parts, seq_in(h1), go[0], n2g, wo))
    n1_own = rows_at(n1, r * rows, rows)
    q_own = seq_out((jnp.dot(seq_in(n1_own), wq, preferred_element_type=F32) + qb_all.astype(F32)).astype(BF16))
    ns_swapped = [core_swap(arrive(x)) for x in ns]
    ub = jnp.zeros((n * units,), F32)
    for k in range(wins):
        part = sum(gsums[s][k] for s in range(group)).reshape(units)
        ub = lax.dynamic_update_slice(ub, part, (tp_at(-k * group) * units,))
    out_g = Grad([[gm]], [[att_own]])
    for k in range(wins):
        ffn_grad(k)
    row0 = r * rows
    d_own = rows_at(dcol, row0, rows).reshape(1, rows)
    keys_t = keys.T

    def heads_back(part):
        return seq_out(attn_bwd(part, 2, row0.reshape(1), seq_in(q_own), gatt, keys, values, keys_t, dcol, d_own, hd))

    back = [heads_back(0)]
    total = seq_in(h1) + down_bias.astype(F32)
    for sp in sum_parts:
        total = total + sp.astype(F32)
    total = seq_out(total.astype(BF16))
    output = lax.all_gather(total, "tp", axis=0, tiled=True)
    back.append(heads_back(1))
    gq = jnp.concatenate([x[0] for x in back], axis=1)
    gk, gv = back[0][1] + back[1][1], back[0][2] + back[1][2]
    gkv_part = jnp.concatenate([gk, gv], axis=1)
    gkv = rows_at(gkv_part, row0, rows)
    kv_got = [group_shift(rows_at(gkv_part, lax.rem(r + s, group) * rows, rows).astype(BF16), s) for s in range(1, group)]
    for k in range(1, wins):
        ffn[k].keep()
        ffn[k].go()
    for got in kv_got:
        gkv = gkv + arrive(got).astype(F32)
    gkv = gkv.astype(BF16)
    gt, sums1, small = seq_out(norm1_back(seq_in(gq), gkv, wq, keyval_weight, x_own, gh1, n1g))
    qkv_g = Grad([[n1_own]], [[jnp.concatenate([gq, gkv], axis=1)]])
    grad_tokens = lax.all_gather(gt, "tp", axis=0, tiled=True)

    pack = jnp.concatenate(
        [sums2[:4].reshape(-1), sums1[:3].reshape(-1), jnp.pad(small[0, hd:], (0, d - hd)), ub]
    )
    swaps = [dict(to_dp=lambda a, s=1 << i: a ^ s) for i in range(ndp.bit_length() - 1)]
    flying = None

    def swap_small():
        nonlocal pack, flying
        if flying is not None:
            pack = seq_out(pack + arrive(flying))
            flying = None
        if swaps:
            flying = perm(pack, **swaps.pop(0))

    swap_small()
    out_g.keep()
    swap_small()
    for k in range(1, wins):
        ffn[k].stage()
    ffn[0].keep()
    swap_small()
    far = [tp_shift(ffn[k].finish(), -k * group) for k in range(1, wins)]
    qkv_g.keep()
    while swaps:
        swap_small()
    swap_small()
    pack_got = [pack] + [tp_shift(pack, s) for s in range(1, n)]
    out_g.go()
    qkv_g.go()
    ffn[0].go()
    out_g.stage()
    qkv_g.stage()
    ffn[0].stage()
    output = seq_out(copied(arrive(output)))
    grad_tokens = seq_out(copied(arrive(grad_tokens)))
    far_up, far_down = 0.0, 0.0
    for got in far:
        got = arrive(got).astype(F32)
        far_up, far_down = seq_out([far_up + got[0], far_down + got[1]])
    g_out = out_g.finish()[0]
    g_qkv = qkv_g.finish()[0]
    f0 = ffn[0].finish()

    take_cols = lambda x, i: lax.dynamic_slice_in_dim(x, i * lq, lq, axis=1)
    kv_rows = g_qkv.shape[0] // n
    fr = g_qkv.shape[0]

    def share(i):
        kv_part = rows_at(g_qkv[:, n * lq :], i * kv_rows, kv_rows)
        return [take_cols(g_out, i), take_cols(g_qkv, i), kv_part.reshape(-1, lq)]

    mine = share(ti)
    shares = [tp_shift(jnp.concatenate(share(tp_at(s)), axis=0), s) for s in range(1, n)]
    g_upw = seq_out(f0[0].astype(F32) + far_up)
    g_downw = seq_out((f0[1].astype(F32) + far_down).T).T
    g_outw, g_qw, g_kvw = [x.astype(F32) for x in mine]
    for got in shares:
        got = arrive(got).astype(F32)
        g_outw = g_outw + got[:fr]
        g_qw = g_qw + got[fr : 2 * fr]
        g_kvw = g_kvw + got[2 * fr :]
    g_outw = seq_out(g_outw.T)
    g_kvw = g_kvw.reshape(kv_rows, -1)
    pack = jnp.zeros_like(pack)
    for j in range(n):
        part = jnp.zeros_like(pack)
        for s in range(n):
            part = part + jnp.where(tp_at(-s) == j, arrive(pack_got[s]), 0.0)
        pack = pack + part
    pack = seq_out(pack)
    piece = lambda row, at, size: lax.dynamic_slice_in_dim(pack, row * d + at, size)
    vs = d // ndp
    qs = lq // ndp
    us = units // ndp
    bs = hd // (ndp * n)
    return (
        output,
        grad_tokens,
        piece(4, m * vs, vs),
        piece(5, m * vs, vs),
        g_qw,
        piece(6, ti * lq + m * qs, qs),
        g_kvw,
        piece(7, (m * n + ti) * bs, bs),
        g_outw,
        piece(2, m * vs, vs),
        piece(0, m * vs, vs),
        piece(1, m * vs, vs),
        g_upw,
        piece(8, ti * units + m * us, us),
        g_downw.T,
        piece(3, m * vs, vs),
    )


def solution(mesh):
    n = mesh.shape["tp"]
    ndp = mesh.shape["dp"]
    return jax.shard_map(
        functools.partial(per_device, n, ndp),
        mesh=mesh,
        in_specs=(
            P("dp", None),
            P("dp", None),
            P(),
            P(),
            P(None, "tp"),
            P("tp"),
            P(),
            P(),
            P("tp", None),
            P(),
            P(),
            P(),
            P(None, "tp"),
            P("tp"),
            P("tp", None),
            P(),
            P("dp", None),
        ),
        out_specs=(
            P("dp", None),
            P("dp", None),
            P("dp"),
            P("dp"),
            P("dp", "tp"),
            P(("tp", "dp")),
            P(("dp", "tp"), None),
            P(("dp", "tp")),
            P("tp", "dp"),
            P("dp"),
            P("dp"),
            P("dp"),
            P("dp", "tp"),
            P(("tp", "dp")),
            P("tp", "dp"),
            P("dp"),
        ),
        check_vma=False,
    )
```

```python
import functools
import math

import jax
import jax.numpy as jnp
from jax import lax
from jax.experimental import pallas as pl
from jax.experimental.pallas import tpu as pltpu
from jax.sharding import PartitionSpec as P

F32 = jnp.float32
BF16 = jnp.bfloat16
NEG = -1e30
EPS = 1e-05
GELU_A = math.sqrt(2.0 / math.pi)
GELU_B = 0.044715
LOG2E = math.log2(math.e)
VMEM_LIMIT = 56 * 1024 * 1024


def dot_nn(a, b):
    return lax.dot_general(a, b, (((1,), (0,)), ((), ())), preferred_element_type=F32)


def dot_nt(a, b):
    return lax.dot_general(a, b, (((1,), (1,)), ((), ())), preferred_element_type=F32)


def dot_tn(a, b):
    return lax.dot_general(a, b, (((0,), (0,)), ((), ())), preferred_element_type=F32)


def call(kernel, grid, in_specs, out_specs, out_shape, scratch=(), prefetch=0, flops=0, nbytes=0, trans=0, name=None):
    return pl.pallas_call(
        kernel,
        grid_spec=pltpu.PrefetchScalarGridSpec(
            num_scalar_prefetch=prefetch,
            grid=grid,
            in_specs=in_specs,
            out_specs=out_specs,
            scratch_shapes=list(scratch),
        ),
        out_shape=out_shape,
        compiler_params=pltpu.CompilerParams(
            dimension_semantics=("arbitrary",) * len(grid), vmem_limit_bytes=VMEM_LIMIT
        ),
        cost_estimate=pl.CostEstimate(flops=flops, bytes_accessed=nbytes, transcendentals=trans),
        name=name,
    )


def whole(shape):
    return pl.BlockSpec(shape, lambda *_: (0,) * len(shape), pipeline_mode=pl.Buffered(1))


def shape_of(shape, dtype):
    return jax.ShapeDtypeStruct(shape, dtype)


def ln_kernel(win_ref, x_ref, g_ref, b_ref, o_ref):
    x = x_ref[...].astype(F32)
    c = x - jnp.mean(x, axis=-1, keepdims=True)
    v = jnp.mean(c * c, axis=-1, keepdims=True)
    o_ref[...] = (c * lax.rsqrt(v + EPS) * g_ref[...].astype(F32) + b_ref[...].astype(F32)).astype(BF16)


def layer_norm(win, x, gain, bias, t):
    d = x.shape[1]
    br = 256
    return call(
        ln_kernel,
        (t // br,),
        [pl.BlockSpec((br, d), lambda i, win_ref: (win_ref[0] * (t // br) + i, 0)), whole((1, d)), whole((1, d))],
        pl.BlockSpec((br, d), lambda i, *_: (i, 0)),
        shape_of((t, d), BF16),
        prefetch=1,
        flops=8 * t * d,
        nbytes=4 * t * d,
        name="norm1",
    )(win, x, gain, bias)


def attn_fwd_kernel(scale, qb, q_ref, k_ref, vt_ref, dcol_ref, drow_ref, o_ref, mask):
    s = q_ref.shape[0]
    reach = s // 2

    def span(j):
        start = max(0, j * qb - reach)
        return start, (j + 1) * qb

    @pl.when(pl.program_id(1) == 0)
    def _():
        for j in range(s // qb):
            lo, hi = span(j)
            kpos = lo + lax.broadcasted_iota(jnp.int32, (hi - lo, qb), 0)
            qpos = j * qb + lax.broadcasted_iota(jnp.int32, (hi - lo, qb), 1)
            ok = (dcol_ref[pl.ds(lo, hi - lo), :] == drow_ref[0, :, pl.ds(j * qb, qb)]) & (kpos <= qpos)
            mask[j, pl.ds(0, hi - lo), :] = jnp.where(ok, 0.0, NEG)

    for j in range(s // qb):
        lo, hi = span(j)
        q = q_ref[pl.ds(j * qb, qb), :]
        sc = dot_nt(k_ref[pl.ds(lo, hi - lo), :], q) + mask[j, pl.ds(0, hi - lo), :]
        top = jnp.max(sc, axis=0, keepdims=True)
        p = jnp.exp2((sc - top) * (scale * LOG2E))
        total = jnp.sum(p, axis=0, keepdims=True)
        o = dot_nn(vt_ref[:, pl.ds(lo, hi - lo)], p.astype(BF16)) / total
        o_ref[pl.ds(j * qb, qb), :] = o.T.astype(BF16)


def attn_fwd(q, k, vt, dcol, drow, seq, hd):
    t, width = q.shape
    heads = width // hd
    qb = 256
    wins = t // seq
    return call(
        functools.partial(attn_fwd_kernel, hd**-0.5, qb),
        (wins, heads),
        [
            pl.BlockSpec((seq, hd), lambda w, h: (w, h)),
            pl.BlockSpec((seq, hd), lambda w, h: (w, 0)),
            pl.BlockSpec((hd, seq), lambda w, h: (0, w)),
            pl.BlockSpec((seq, 1), lambda w, h: (w, 0)),
            pl.BlockSpec((1, 1, seq), lambda w, h: (w, 0, 0)),
        ],
        pl.BlockSpec((seq, hd), lambda w, h: (w, h)),
        shape_of((t, width), BF16),
        scratch=[pltpu.VMEM((seq // qb, seq // 2 + qb, qb), F32)],
        flops=4 * t * seq * width * 5 // 8,
        nbytes=4 * t * width + 4 * t * hd,
        trans=t * seq * heads * 5 // 8,
        name="attn_fwd",
    )(q, k, vt, dcol, drow)


def proj_ln_kernel(att_ref, w_ref, x_ref, ob_ref, g_ref, b_ref, h_ref, n_ref):
    att = att_ref[...]
    mixed = jnp.concatenate([dot_nn(att, w_ref[i]) for i in range(w_ref.shape[0])], axis=1)
    h = x_ref[...].astype(F32) + mixed + ob_ref[...].astype(F32)
    h_ref[...] = h
    c = h - jnp.mean(h, axis=-1, keepdims=True)
    v = jnp.mean(c * c, axis=-1, keepdims=True)
    n_ref[...] = (c * lax.rsqrt(v + EPS) * g_ref[...].astype(F32) + b_ref[...].astype(F32)).astype(BF16)


def proj_ln(att, w, x, out_bias, gain, bias):
    r, width = att.shape
    d = x.shape[1]
    br = min(256, r)
    row = pl.BlockSpec((br, d), lambda i: (i, 0))
    return call(
        proj_ln_kernel,
        (r // br,),
        [pl.BlockSpec((br, width), lambda i: (i, 0)), whole(w.shape), row] + [whole((1, d))] * 3,
        [row, row],
        [shape_of((r, d), F32), shape_of((r, d), BF16)],
        flops=2 * r * width * d,
        nbytes=2 * width * d + 10 * r * d,
        name="proj_ln",
    )(att, w, x, out_bias, gain, bias)


def gelu_parts(v):
    v2 = v * v
    g = 1.0 / (1.0 + jnp.exp2(v * (-2.0 * GELU_A * LOG2E * (1.0 + GELU_B * v2))))
    return v * g, g + v * (g * (1.0 - g)) * (2.0 * GELU_A * (1.0 + 3.0 * GELU_B * v2))


def up_kernel(ready, n_ref, w_ref, b_ref, *refs):
    r = n_ref.shape[0]
    parts = 2 if ready else 1
    pair_ref, gs_ref = refs[-2:]
    total = None
    for i in range(parts):
        at = pl.ds(i * (r // parts), r // parts)
        v = dot_nn(n_ref[at, :], w_ref[...]) + b_ref[...].astype(F32)
        da = refs[0][at, :].astype(F32) if ready else dot_nt(refs[0][at, :], refs[1][...])
        act, slope = gelu_parts(v)
        pair_ref[0, at, :] = act.astype(BF16)
        gb = (da * slope).astype(BF16)
        pair_ref[1, at, :] = gb
        part = jnp.sum(gb.astype(F32), axis=0, keepdims=True)
        total = part if total is None else total + part
    gs_ref[...] = total


def ffn_up(n, w, b, da=None, go=None, down=None):
    r, d = n.shape
    u = w.shape[1]
    ready = da is not None
    bn = min(512 if ready else 256, u)
    col = pl.BlockSpec((r, bn), lambda j: (0, j))
    line = pl.BlockSpec((1, bn), lambda j: (0, j))
    extra = [col] if ready else [whole((r, d)), pl.BlockSpec((bn, d), lambda j: (j, 0))]
    return call(
        functools.partial(up_kernel, ready),
        (u // bn,),
        [whole((r, d)), pl.BlockSpec((d, bn), lambda j: (0, j)), line] + extra,
        [pl.BlockSpec((2, r, bn), lambda j: (0, 0, j)), line],
        [shape_of((2, r, u), BF16), shape_of((1, u), F32)],
        flops=(2 if ready else 4) * r * d * u,
        nbytes=2 * d * u + 6 * r * u + 2 * r * d,
        trans=r * u,
        name="ffn_up",
    )(n, w, b, *((da,) if ready else (go, down)))


def product_kernel(count, nt, *refs):
    acc = None
    for x, w in zip(refs[:count], refs[count : 2 * count]):
        part = (dot_nt if nt else dot_nn)(x[...], w[...])
        acc = part if acc is None else acc + part
    refs[-1][...] = acc.astype(BF16)


def plane(x, i):
    return pl.BlockSpec((None,) + x.shape[1:], lambda *_: (i, 0, 0), pipeline_mode=pl.Buffered(1))


def product(xs, at, ws, nt):
    r, k = xs[0].shape[1:]
    n = ws[0].shape[0 if nt else 1]
    bn = 512
    wspec = pl.BlockSpec((bn, k), lambda j: (j, 0)) if nt else pl.BlockSpec((k, bn), lambda j: (0, j))
    return call(
        functools.partial(product_kernel, len(xs), nt),
        (n // bn,),
        [plane(x, at) for x in xs] + [wspec] * len(xs),
        pl.BlockSpec((r, bn), lambda j: (0, j)),
        shape_of((r, n), BF16),
        flops=2 * r * k * n * len(xs),
        nbytes=len(xs) * 2 * k * (r + n) + 2 * r * n,
        name="product",
    )(*xs, *ws)


def norm2_back_kernel(count, *refs):
    parts = refs[: count]
    h_ref, go_ref, g_ref, w_ref, gh_ref, gm_ref, ga_ref, sums_ref = refs[count:]

    @pl.when(pl.program_id(0) == 0)
    def _():
        sums_ref[...] = jnp.zeros_like(sums_ref)

    gn = parts[0][...].astype(F32)
    for part in parts[1:]:
        gn = gn + part[...].astype(F32)
    h = h_ref[...]
    c = h - jnp.mean(h, axis=-1, keepdims=True)
    inv = lax.rsqrt(jnp.mean(c * c, axis=-1, keepdims=True) + EPS)
    nrm = c * inv
    u = gn * g_ref[...].astype(F32)
    cot = go_ref[...].astype(F32)
    gh = cot + inv * (u - jnp.mean(u, axis=-1, keepdims=True) - nrm * jnp.mean(u * nrm, axis=-1, keepdims=True))
    gh_ref[...] = gh
    gm = gh.astype(BF16)
    gm_ref[...] = gm
    cols = w_ref.shape[2]
    ga = dot_nt(gm[:, :cols], w_ref[0])
    for i in range(1, w_ref.shape[0]):
        ga = ga + dot_nt(gm[:, i * cols : (i + 1) * cols], w_ref[i])
    ga_ref[...] = ga.astype(BF16)
    sums_ref[0:1, :] += jnp.sum(gn * nrm, axis=0, keepdims=True)
    sums_ref[1:2, :] += jnp.sum(gn, axis=0, keepdims=True)
    sums_ref[2:3, :] += jnp.sum(gh, axis=0, keepdims=True)
    sums_ref[3:4, :] += jnp.sum(cot, axis=0, keepdims=True)


def norm2_back(parts, h, go, gain, w):
    r, d = h.shape
    width = w.shape[1]
    br = min(256, r)
    row = pl.BlockSpec((br, d), lambda i: (i, 0))
    wide = pl.BlockSpec((br, width), lambda i: (i, 0))
    return call(
        functools.partial(norm2_back_kernel, len(parts)),
        (r // br,),
        [row] * len(parts) + [row, row, whole((1, d)), whole(w.shape)],
        [row, row, wide, pl.BlockSpec((8, d), lambda i: (0, 0))],
        [shape_of((r, d), F32), shape_of((r, d), BF16), shape_of((r, width), BF16), shape_of((8, d), F32)],
        flops=2 * r * width * d,
        nbytes=2 * width * d + 20 * r * d,
        name="norm2_back",
    )(*parts, h, go, gain, w)


def attn_bwd_kernel(scale, qb, reach, row0_ref, q_ref, go_ref, k_ref, v_ref, kt_ref, dcol_ref, drow_ref, gq_ref, gk_ref, gv_ref, mask):
    rows = q_ref.shape[0]
    span = reach + qb
    first = pl.program_id(0) == 0

    def start(j):
        at = jnp.maximum(row0_ref[0] + j * qb - reach, 0)
        return pl.multiple_of(at, qb)

    @pl.when(first)
    def _():
        gk_ref[...] = jnp.zeros_like(gk_ref)
        gv_ref[...] = jnp.zeros_like(gv_ref)
        for j in range(rows // qb):
            lo = start(j)
            kpos = lo + lax.broadcasted_iota(jnp.int32, (span, qb), 0)
            qpos = row0_ref[0] + j * qb + lax.broadcasted_iota(jnp.int32, (span, qb), 1)
            ok = (dcol_ref[pl.ds(lo, span), :] == drow_ref[:, pl.ds(j * qb, qb)]) & (kpos <= qpos)
            mask[j] = jnp.where(ok, 0.0, NEG)

    for j in range(rows // qb):
        lo = start(j)
        q = q_ref[pl.ds(j * qb, qb), :]
        go = go_ref[pl.ds(j * qb, qb), :]
        k = k_ref[pl.ds(lo, span), :]
        sc = dot_nt(k, q) + mask[j]
        top = jnp.max(sc, axis=0, keepdims=True)
        e = jnp.exp2((sc - top) * (scale * LOG2E))
        p = e * (1.0 / jnp.sum(e, axis=0, keepdims=True))
        dp = dot_nt(v_ref[pl.ds(lo, span), :], go)
        pd = p * dp
        delta = jnp.sum(pd, axis=0, keepdims=True)
        ds = ((pd - p * delta) * scale).astype(BF16)
        gk_ref[pl.ds(lo, span), :] += dot_nn(ds, q)
        gv_ref[pl.ds(lo, span), :] += dot_nn(p.astype(BF16), go)
        gq_ref[pl.ds(j * qb, qb), :] = dot_nn(kt_ref[:, pl.ds(lo, span)], ds).T.astype(BF16)


def attn_bwd(part, parts, row0, q, go, k, v, kt, dcol, drow, hd):
    r, width = q.shape[0], q.shape[1] // parts
    s = k.shape[0]
    heads = width // hd
    qb = min(256, r)
    reach = s // 2
    head = pl.BlockSpec((r, hd), lambda h, *_: (0, h))
    head_in = pl.BlockSpec((r, hd), lambda h, *_: (0, h + part * heads))
    keep = pl.BlockSpec((s, hd), lambda h, *_: (0, 0))
    return call(
        functools.partial(attn_bwd_kernel, hd**-0.5, qb, reach),
        (heads,),
        [head_in, head_in, whole((s, hd)), whole((s, hd)), whole((hd, s)), whole((s, 1)), whole((1, r))],
        [head, keep, keep],
        [shape_of((r, width), BF16), shape_of((s, hd), F32), shape_of((s, hd), F32)],
        scratch=[pltpu.VMEM((r // qb, reach + qb, qb), F32)],
        prefetch=1,
        flops=10 * r * (reach + qb) * width,
        nbytes=6 * r * width + 16 * s * hd,
        trans=r * (reach + qb) * heads,
        name="attn_bwd",
    )(row0, q, go, k, v, kt, dcol, drow)


def norm1_back_kernel(gq_ref, gkv_ref, wq_ref, wkv_ref, x_ref, gh_ref, g_ref, gt_ref, sums_ref, small_ref):
    @pl.when(pl.program_id(0) == 0)
    def _():
        sums_ref[...] = jnp.zeros_like(sums_ref)
        small_ref[...] = jnp.zeros_like(small_ref)

    gq = gq_ref[...]
    gkv = gkv_ref[...]
    gn = dot_nt(gq, wq_ref[...]) + dot_nt(gkv, wkv_ref[...])
    x = x_ref[...].astype(F32)
    c = x - jnp.mean(x, axis=-1, keepdims=True)
    inv = lax.rsqrt(jnp.mean(c * c, axis=-1, keepdims=True) + EPS)
    nrm = c * inv
    u = gn * g_ref[...].astype(F32)
    gx = inv * (u - jnp.mean(u, axis=-1, keepdims=True) - nrm * jnp.mean(u * nrm, axis=-1, keepdims=True))
    gt_ref[...] = (gh_ref[...] + gx).astype(BF16)
    sums_ref[0:1, :] += jnp.sum(gn * nrm, axis=0, keepdims=True)
    sums_ref[1:2, :] += jnp.sum(gn, axis=0, keepdims=True)
    sums_ref[2:3, :] += jnp.sum(gq.astype(F32), axis=0, keepdims=True)
    small_ref[0:1, :] += jnp.sum(gkv.astype(F32), axis=0, keepdims=True)


def norm1_back(gq, gkv, wq, wkv, x, gh, gain):
    r, d = x.shape
    br = min(256, r)
    row = pl.BlockSpec((br, d), lambda i: (i, 0))
    kvw = gkv.shape[1]
    return call(
        norm1_back_kernel,
        (r // br,),
        [row, pl.BlockSpec((br, kvw), lambda i: (i, 0)), whole(wq.shape), whole(wkv.shape), row, row, whole((1, d))],
        [row, pl.BlockSpec((8, d), lambda i: (0, 0)), pl.BlockSpec((8, kvw), lambda i: (0, 0))],
        [shape_of((r, d), BF16), shape_of((8, d), F32), shape_of((8, kvw), F32)],
        flops=2 * r * d * (gq.shape[1] + kvw),
        nbytes=2 * d * (gq.shape[1] + kvw) + 12 * r * d,
        name="norm1_back",
    )(gq, gkv, wq, wkv, x, gh, gain)


def stage_orders(bits):
    order = list(range(bits))
    return [order, order[1:] + order[:1]]


def place_in(p, bits, order):
    rel = {bit: (p >> (bits - 1 - k)) & 1 for k, bit in enumerate(range(bits))}
    out = 0
    for bit in order:
        out = 2 * out + rel[bit]
    return out


def table(p, values):
    out = values[0]
    for i, v in enumerate(values[1:], 1):
        out = jnp.where(p == i, v, out)
    return out


def grad_kernel(count, pairs, places, m_ref, *refs):
    lefts = [refs[i * count : (i + 1) * count] for i in range(pairs)]
    rights = [refs[(pairs + i) * count : (pairs + i + 1) * count] for i in range(pairs)]
    outs = refs[2 * pairs * count :]
    bits = places.bit_length() - 1
    p = pl.program_id(1)
    cut = rights[0][0].shape[1] // 2

    def run(left, right):
        acc = dot_tn(left[0][...], right[0][...])
        for a, b in zip(left[1:], right[1:]):
            acc = acc + dot_tn(a[...], b[...])
        acc = acc.astype(BF16)
        for h, order in enumerate(stage_orders(bits)):
            sent = [place_in(i, bits, order) < places // 2 for i in range(places)]
            here = table(p, sent)
            send_ref, keep_ref = outs[2 * h], outs[2 * h + 1]
            part = acc[:, h * cut : (h + 1) * cut]

            @pl.when(here)
            def _(send_ref=send_ref, part=part):
                send_ref[0, 0] = part

            @pl.when(jnp.logical_not(here))
            def _(keep_ref=keep_ref, part=part):
                keep_ref[0, 0] = part

    for i in range(pairs):
        pl.when(pl.program_id(0) == i)(functools.partial(run, lefts[i], rights[i]))


def grad_call(m, ndp, lefts, rights):
    pairs, count = len(lefts), len(lefts[0])
    d, n = lefts[0][0].shape[1], rights[0][0][0].shape[2]
    places = ndp // 2
    bits = places.bit_length() - 1
    hp = places // 2
    f = d // ndp

    def left_map(own, i, p, m_ref):
        me = m_ref[0]
        p = jnp.where(i < own, 0, jnp.where(i > own, places - 1, p))
        b = 0
        for k in range(bits):
            b = b + ((((p >> (bits - 1 - k)) & 1) ^ 1 ^ ((me >> (k + 1)) & 1)) << k)
        return (0, 2 * b + (me & 1))

    specs = [pl.BlockSpec((a.shape[0], f), functools.partial(left_map, i)) for i in range(pairs) for a in lefts[i]]
    specs += [plane(b, at) for i in range(pairs) for b, at in rights[i]]
    outs, shapes = [], []
    for order in stage_orders(bits):
        at = [place_in(i, bits, order) for i in range(places)]
        for first in (0, hp):
            seen = [next((a - first for a in at[: i + 1][::-1] if 0 <= a - first < hp), None) for i in range(places)]
            start = next(a for a in seen if a is not None)
            seen = [start if a is None else a for a in seen]
            outs.append(pl.BlockSpec((1, 1, f, n // 2), lambda i, p, *_, seen=seen: (i, table(p, seen), 0, 0)))
            shapes.append(shape_of((pairs, hp, f, n // 2), BF16))
    k = sum(a.shape[0] for a in lefts[0]) * pairs
    return call(
        functools.partial(grad_kernel, count, pairs, places),
        (pairs, places),
        specs,
        outs,
        shapes,
        prefetch=1,
        flops=k * d * n,
        nbytes=k * d + 2 * k * n + pairs * d * n,
        name="weight_grad",
    )(m, *[a for l in lefts for a in l], *[b for r in rights for b, _ in r])


def copy_kernel(x_ref, o_ref):
    o_ref[...] = x_ref[...]


def copied(x):
    t, d = x.shape
    br = 256
    row = pl.BlockSpec((br, d), lambda i: (i, 0))
    return call(copy_kernel, (t // br,), [row], row, shape_of((t, d), x.dtype), nbytes=4 * t * d, name="copied")(x)


def per_device(
    n,
    ndp,
    tokens,
    doc_ids,
    norm1_gain,
    norm1_bias,
    query_weight,
    query_bias,
    keyval_weight,
    value_bias,
    out_weight,
    out_bias,
    norm2_gain,
    norm2_bias,
    up_weight,
    up_bias,
    down_weight,
    down_bias,
    grad_out,
):
    t_all, d = tokens.shape
    wins, seq = doc_ids.shape
    hd = value_bias.shape[0]
    lq = query_weight.shape[1]
    units = up_weight.shape[1]
    group = n // wins
    rows = t_all // n
    ti = lax.axis_index("tp")
    m = lax.axis_index("dp")
    mv = m.reshape(1)
    r = lax.rem(ti, group)
    win = lax.div(ti, group)
    tok = [None]

    def perm(x, to_dp=lambda a: a, to_tp=lambda a: a):
        pairs = [(a * n + b, to_dp(a) * n + to_tp(b)) for a in range(ndp) for b in range(n)]
        return lax.ppermute(x, ("dp", "tp"), pairs)

    def tp_shift(x, s):
        return perm(x, to_tp=lambda b: (b + s) % n)

    def group_shift(x, s):
        return perm(x, to_tp=lambda b: (b // group) * group + (b + s) % group)

    def tp_at(s):
        return lax.rem(ti + (s % n), n)

    def after(x, *marks):
        return lax.optimization_barrier((x,) + marks)[0]

    def seq_in(x):
        return x if tok[0] is None else after(x, tok[0])

    def seq_out(x):
        tok[0] = x[0] if isinstance(x, (tuple, list)) else x
        return x

    def rows_at(x, start, size):
        return lax.dynamic_slice_in_dim(x, start, size, axis=0)

    vec = lambda v: v.reshape(1, -1)
    n1g, n1b, n2g, n2b = vec(norm1_gain), vec(norm1_bias), vec(norm2_gain), vec(norm2_bias)

    def spread(piece, axis):
        size = piece.shape[axis]
        shape = list(piece.shape)
        shape[axis] = n * size
        full = jnp.zeros(shape, piece.dtype)
        for s in range(n):
            got = piece if s == 0 else tp_shift(piece, s)
            at = [0, 0]
            at[axis] = tp_at(-s) * size
            full = lax.dynamic_update_slice(full, got, at)
        return full

    slab = d // ndp
    uslab = units // ndp

    def arrive(x):
        return after(x, tok[0])

    def core_swap(x):
        return perm(x, to_dp=lambda a: a ^ 1)

    def spread_send(piece):
        return [piece] + [tp_shift(piece, s) for s in range(1, n)]

    def spread_place(gots, axis):
        size = gots[0].shape[axis]
        shape = list(gots[0].shape)
        shape[axis] = n * size
        full = jnp.zeros(shape, gots[0].dtype)
        for s in range(n):
            at = [0, 0]
            at[axis] = tp_at(-s) * size
            full = lax.dynamic_update_slice(full, gots[s] if s == 0 else arrive(gots[s]), at)
        return seq_out(full)

    def with_bias(piece, bias):
        return jnp.concatenate([piece, jnp.broadcast_to(bias.reshape(1, -1), (16, bias.shape[0]))], axis=0)

    wq_slab = with_bias(rows_at(query_weight, m * slab, slab), query_bias)
    wq_far = [tp_shift(wq_slab, t * group) for t in range(1, wins)]
    qb_far = [a[slab] for a in wq_far]
    wo_got = spread_send(lax.dynamic_slice_in_dim(out_weight, m * slab, slab, axis=1))
    n1 = seq_out(layer_norm(win.reshape(1), tokens, n1g, n1b, seq))
    kv = seq_out(jnp.dot(n1, keyval_weight, preferred_element_type=F32))
    keys = kv[:, :hd].astype(BF16)
    values = (kv[:, hd:] + value_bias.astype(F32)).astype(BF16)
    values_t = values.T
    dcol = rows_at(doc_ids, win, 1).reshape(seq, 1)
    drow = rows_at(doc_ids, win, 1).reshape(1, 1, seq)
    wq_far = [lax.all_gather(after(a[:slab], kv), "dp", axis=0, tiled=True) for a in wq_far]
    go = [rows_at(grad_out, (win * group + lax.rem(r + group - s, group)) * rows, rows) for s in range(group)]
    das = []

    def grad_act(s):
        das.append(seq_out(lax.dot_general(seq_in(go[s]), down_weight, (((1,), (1,)), ((), ())), preferred_element_type=F32).astype(BF16)))

    def heads(w, b):
        q = seq_out((jnp.dot(seq_in(n1), w, preferred_element_type=F32) + b.astype(F32)).astype(BF16))
        att = seq_out(attn_fwd(q, keys, values_t, dcol, drow, seq, hd))
        got = [rows_at(att, r * rows, rows)]
        return got + [group_shift(rows_at(att, lax.rem(r + s, group) * rows, rows), s) for s in range(1, group)]

    up_slab = with_bias(rows_at(up_weight, m * slab, slab), up_bias)
    up_far = [tp_shift(after(up_slab, kv), t * group) for t in range(1, wins)]
    att_got = [heads(query_weight, query_bias)]
    wo_z = spread_place(wo_got, 0)
    wo = lax.all_gather(wo_z, "dp", axis=0, tiled=False)
    down_far = [tp_shift(after(rows_at(down_weight, m * uslab, uslab), wo_z), t * group) for t in range(1, wins)]
    for w, b in zip(wq_far, qb_far):
        att_got.append(heads(w, b))
    upb_far = [a[slab : slab + 1] for a in up_far]
    up_far = [lax.all_gather(arrive(a)[:slab], "dp", axis=0, tiled=True) for a in up_far]
    att_own = jnp.zeros((rows, n * lq), BF16)
    for t in range(wins):
        if t == wins - 1:
            for s in range(group):
                grad_act(s)
        for s in range(group):
            col = lax.rem(win * group + lax.rem(r + group - s, group) + n - t * group, n) * lq
            att_own = seq_out(lax.dynamic_update_slice(att_own, arrive(att_got[t][s]), (0, col)))
    x_own = rows_at(tokens, ti * rows, rows)
    h1, n2 = seq_out(proj_ln(att_own, wo, x_own, vec(out_bias), n2g, n2b))

    ns = [n2] + [group_shift(n2, s) for s in range(1, group)]
    down_far = [lax.all_gather(after(b, h1), "dp", axis=0, tiled=True) for b in down_far]
    ups, downs = [up_weight] + up_far, [down_weight] + down_far
    upbs = [vec(up_bias)] + upb_far
    units_of = [[None] * wins for _ in range(group)]
    gsums = [[None] * wins for _ in range(group)]

    def up(s, k):
        x = seq_in(ns[s])
        res = ffn_up(x, ups[k], upbs[k], da=das[s]) if k == 0 else ffn_up(x, ups[k], upbs[k], go=go[s], down=downs[k])
        units_of[s][k], gsums[s][k] = seq_out(res)

    def back_up(s):
        return seq_out(product([seq_in(units_of[s][0])] + units_of[s][1:], 1, ups, True))

    def down(s):
        return seq_out(product([seq_in(units_of[s][0])] + units_of[s][1:], 0, downs, False))

    class Grad:
        def __init__(self, lefts, rights):
            self.lefts = [l + [core_swap(arrive(a)) for a in l] for l in lefts]
            self.rights = [[(a[None], 0) for a in x + [core_swap(arrive(a)) for a in x]] for x in rights]

        def keep(self):
            lefts = [[seq_in(self.lefts[0][0])] + self.lefts[0][1:]] + self.lefts[1:]
            res = seq_out(grad_call(mv, ndp, lefts, self.rights))
            self.orders = [list(o) for o in stage_orders((ndp // 2).bit_length() - 1)]
            self.res = res

        def go(self):
            self.halves = [self.leave(h, arrive(self.res[2 * h]), self.res[2 * h + 1]) for h in range(2)]

        def leave(self, h, send, keep):
            b = self.orders[h].pop(0)
            return keep, perm(send, to_dp=lambda a: a ^ (2 << b))

        def stage(self):
            nxt = []
            for h in range(2):
                keep, got = self.halves[h]
                x = seq_out((keep.astype(F32) + arrive(got).astype(F32)).astype(BF16))
                half = x.shape[1] // 2
                nxt.append(self.leave(h, x[:, :half], x[:, half:]) if half else x[:, 0])
            self.halves = nxt

        def finish(self):
            while self.orders[0]:
                self.stage()
            self.stage()
            return jnp.concatenate(self.halves, axis=2)

    go_swapped = [core_swap(after(g, n1)) for g in go]

    late = list(range(1, group)) + [0]
    gn2_parts, sum_parts = [None] * group, [None] * group

    up(0, 0)
    for s in range(1, group):
        up(s, 0)
    wq_got = spread_send(after(wq_slab, *ns))
    for s in late:
        for k in range(1, wins):
            up(s, k)
        if s == late[0]:
            wq_z = spread_place(wq_got, 1)
            qb_all = wq_z[slab]
            wq = lax.all_gather(wq_z[:slab], "dp", axis=0, tiled=True)
        part = back_up(s)
        gn2_parts[s] = part if s == 0 else group_shift(part, -s)
    for s in late:
        part = down(s)
        sum_parts[s] = part if s == 0 else group_shift(part, -s)
    ffn = []

    def ffn_grad(k):
        g = Grad([], [])
        g.lefts = [ns + ns_swapped, go + go_swapped]
        both = [units_of[s][k] for s in range(group)]
        both = both + [core_swap(arrive(a)) for a in both]
        g.rights = [[(a, 1) for a in both], [(a, 0) for a in both]]
        ffn.append(g)

    gh1, gm, gatt, sums2 = seq_out(norm2_back(gn2_parts, seq_in(h1), go[0], n2g, wo))
    n1_own = rows_at(n1, r * rows, rows)
    q_own = seq_out((jnp.dot(seq_in(n1_own), wq, preferred_element_type=F32) + qb_all.astype(F32)).astype(BF16))
    ns_swapped = [core_swap(arrive(x)) for x in ns]
    ub = jnp.zeros((n * units,), F32)
    for k in range(wins):
        part = sum(gsums[s][k] for s in range(group)).reshape(units)
        ub = lax.dynamic_update_slice(ub, part, (tp_at(-k * group) * units,))
    out_g = Grad([[gm]], [[att_own]])
    for k in range(wins):
        ffn_grad(k)
    row0 = r * rows
    d_own = rows_at(dcol, row0, rows).reshape(1, rows)
    keys_t = keys.T

    def heads_back(part):
        return seq_out(attn_bwd(part, 2, row0.reshape(1), seq_in(q_own), gatt, keys, values, keys_t, dcol, d_own, hd))

    back = [heads_back(0)]
    total = seq_in(h1) + down_bias.astype(F32)
    for sp in sum_parts:
        total = total + sp.astype(F32)
    total = seq_out(total.astype(BF16))
    output = lax.all_gather(total, "tp", axis=0, tiled=True)
    back.append(heads_back(1))
    gq = jnp.concatenate([x[0] for x in back], axis=1)
    gk, gv = back[0][1] + back[1][1], back[0][2] + back[1][2]
    gkv_part = jnp.concatenate([gk, gv], axis=1)
    gkv = rows_at(gkv_part, row0, rows)
    kv_got = [group_shift(rows_at(gkv_part, lax.rem(r + s, group) * rows, rows).astype(BF16), s) for s in range(1, group)]
    for k in range(1, wins):
        ffn[k].keep()
        ffn[k].go()
    for got in kv_got:
        gkv = gkv + arrive(got).astype(F32)
    gkv = gkv.astype(BF16)
    gt, sums1, small = seq_out(norm1_back(seq_in(gq), gkv, wq, keyval_weight, x_own, gh1, n1g))
    qkv_g = Grad([[n1_own]], [[jnp.concatenate([gq, gkv], axis=1)]])
    grad_tokens = lax.all_gather(gt, "tp", axis=0, tiled=True)

    pack = jnp.concatenate(
        [sums2[:4].reshape(-1), sums1[:3].reshape(-1), jnp.pad(small[0, hd:], (0, d - hd)), ub]
    )
    swaps = [dict(to_dp=lambda a, s=1 << i: a ^ s) for i in range(ndp.bit_length() - 1)]
    flying = None

    def swap_small():
        nonlocal pack, flying
        if flying is not None:
            pack = seq_out(pack + arrive(flying))
            flying = None
        if swaps:
            flying = perm(pack, **swaps.pop(0))

    swap_small()
    out_g.keep()
    swap_small()
    for k in range(1, wins):
        ffn[k].stage()
    ffn[0].keep()
    swap_small()
    far = [tp_shift(ffn[k].finish(), -k * group) for k in range(1, wins)]
    qkv_g.keep()
    while swaps:
        swap_small()
    swap_small()
    pack_got = [pack] + [tp_shift(pack, s) for s in range(1, n)]
    out_g.go()
    qkv_g.go()
    ffn[0].go()
    out_g.stage()
    qkv_g.stage()
    ffn[0].stage()
    g_out = out_g.finish()[0]
    g_qkv = qkv_g.finish()[0]
    f0 = ffn[0].finish()

    take_cols = lambda x, i: lax.dynamic_slice_in_dim(x, i * lq, lq, axis=1)
    kv_rows = g_qkv.shape[0] // n
    fr = g_qkv.shape[0]

    def share(i):
        kv_part = rows_at(g_qkv[:, n * lq :], i * kv_rows, kv_rows)
        return [take_cols(g_out, i), take_cols(g_qkv, i), kv_part.reshape(-1, lq)]

    mine = share(ti)
    shares = [tp_shift(jnp.concatenate(share(tp_at(s)), axis=0), s) for s in range(1, n)]
    output = seq_out(copied(arrive(output)))
    grad_tokens = seq_out(copied(arrive(grad_tokens)))
    g_upw, g_downw = f0[0].astype(F32), f0[1].astype(F32)
    for got in far:
        got = arrive(got).astype(F32)
        g_upw = g_upw + got[0]
        g_downw = g_downw + got[1]
    g_upw = seq_out(g_upw)
    g_downw = seq_out(g_downw.T).T
    g_outw, g_qw, g_kvw = [x.astype(F32) for x in mine]
    for got in shares:
        got = arrive(got).astype(F32)
        g_outw = g_outw + got[:fr]
        g_qw = g_qw + got[fr : 2 * fr]
        g_kvw = g_kvw + got[2 * fr :]
    g_outw = seq_out(g_outw.T)
    g_kvw = g_kvw.reshape(kv_rows, -1)
    pack = jnp.zeros_like(pack)
    for j in range(n):
        part = jnp.zeros_like(pack)
        for s in range(n):
            part = part + jnp.where(tp_at(-s) == j, arrive(pack_got[s]), 0.0)
        pack = pack + part
    pack = seq_out(pack)
    piece = lambda row, at, size: lax.dynamic_slice_in_dim(pack, row * d + at, size)
    vs = d // ndp
    qs = lq // ndp
    us = units // ndp
    bs = hd // (ndp * n)
    return (
        output,
        grad_tokens,
        piece(4, m * vs, vs),
        piece(5, m * vs, vs),
        g_qw,
        piece(6, ti * lq + m * qs, qs),
        g_kvw,
        piece(7, (m * n + ti) * bs, bs),
        g_outw,
        piece(2, m * vs, vs),
        piece(0, m * vs, vs),
        piece(1, m * vs, vs),
        g_upw,
        piece(8, ti * units + m * us, us),
        g_downw.T,
        piece(3, m * vs, vs),
    )


def solution(mesh):
    n = mesh.shape["tp"]
    ndp = mesh.shape["dp"]
    return jax.shard_map(
        functools.partial(per_device, n, ndp),
        mesh=mesh,
        in_specs=(
            P("dp", None),
            P("dp", None),
            P(),
            P(),
            P(None, "tp"),
            P("tp"),
            P(),
            P(),
            P("tp", None),
            P(),
            P(),
            P(),
            P(None, "tp"),
            P("tp"),
            P("tp", None),
            P(),
            P("dp", None),
        ),
        out_specs=(
            P("dp", None),
            P("dp", None),
            P("dp"),
            P("dp"),
            P("dp", "tp"),
            P(("tp", "dp")),
            P(("dp", "tp"), None),
            P(("dp", "tp")),
            P("tp", "dp"),
            P("dp"),
            P("dp"),
            P("dp"),
            P("dp", "tp"),
            P(("tp", "dp")),
            P("tp", "dp"),
            P("dp"),
        ),
        check_vma=False,
    )
```
